128 devices in a mesh: lat: 8 (over x, core), lon: 16 (over y, z).
Axes of the slice: x: 4, y: 4, z: 4, core: 2. Of those that a mesh axis runs over, the one named last changes fastest.
Arguments:
- fields: float32 [4, 90, 128, 2048], P(None, None, 'lat', 'lon'), may hold values from -6 to 6
- courant_lon: float32 [90, 128, 2048], P(None, 'lat', 'lon'), may hold values from -0.3 to 0.3
- courant_lat: float32 [90, 128, 2048], P(None, 'lat', 'lon'), may hold values from -0.3 to 0.3
- diffusion: float32 [90, 128, 2048], P(None, 'lat', 'lon'), may hold values from 0.1 to 0.24
- tend_cot: bfloat16 [4, 90, 128, 2048], P(None, None, 'lat', 'lon'), may hold values from -6 to 6
- col_list: int32 [8, 16, 2048], P('lat', 'lon'), may hold values from 0 to 2047, as said below
- block_count: int32 [8, 16, 16], P('lat', 'lon'), may hold values from 1 to 128, as said below
- block_dest: int32 [8, 16, 16], P('lat', 'lon'), may hold values from 0 to 15, each once within a row
- w_in: bfloat16 [16, 360, 512], P('lon', None, 'lat'), may hold values from -0.3125 to 0.3125
- w_mid: bfloat16 [16, 512, 512], P('lon', None, 'lat'), may hold values from -0.25 to 0.25
- w_out: bfloat16 [16, 360, 512], P('lon', None, 'lat'), may hold values from -0.25 to 0.25
Outputs:
- new_fields: float32 [4, 90, 128, 2048], P(None, None, 'lat', 'lon')
- adjoint: bfloat16 [4, 90, 128, 2048], P(None, None, 'lat', 'lon')
- grad_in: float32 [16, 360, 512], P('lon', None, 'lat')
- grad_mid: float32 [16, 512, 512], P('lon', None, 'lat')
- grad_out: float32 [16, 360, 512], P('lon', None, 'lat')
The draws below stay inside these ranges and needn't reach their ends.
Inputs may be any that keep to these rules, and one draw needn't show every extreme that they name: `col_list`: within one tile's list no local column appears twice. `block_count`: in each tile one block has all 128 slots live. `block_dest`: each tile's row names every expert exactly once.
All inputs are finite; a program needn't handle non-finite values.
Results may differ from the reference program's by a relative error of at most 0.0074.
Values may be sent and summed in bfloat16 or wider, within the bound.
No kernel may reach another device: no remote copies, remote signals or barrier semaphores. Data moves between devices by JAX's collectives and lax.ppermute only.
A program may use at most 320 MiB of HBM per device.

```python
import jax
import jax.numpy as jnp
from jax import lax

LEV = 90
FEAT = 360
HID = 512
CLAT = 16
CLON = 128
BLK = 128
STEPS = 4
NLAT = 128
NLON = 2048
EXPERTS = 16
N_LAT = 8
N_LON = 16


def draw_col_list(key, part):
    keys = jax.random.split(jax.random.fold_in(key, 11), N_LAT * N_LON)

    def one(single):
        return jax.random.permutation(single, CLAT * CLON)[:BLK * N_LON].astype(jnp.int32)
    return jax.vmap(one)(keys).reshape(N_LAT, N_LON, BLK * N_LON)


def draw_block_count(key, part):
    base = jax.random.fold_in(key, 23)
    key_level, key_raw, key_full = jax.random.split(base, 3)
    level = jax.random.randint(key_level, (N_LAT, N_LON, 1), 0, 4)
    raw = jax.random.randint(key_raw, (N_LAT, N_LON, N_LON), 0, 3 * BLK // 4) + level * (BLK // 4) + 1
    full = jax.random.randint(key_full, (N_LAT, N_LON, 1), 0, N_LON)
    index = jnp.arange(N_LON, dtype=jnp.int32)[None, None, :]
    return jnp.where(index == full, BLK, jnp.minimum(raw, BLK)).astype(jnp.int32)


def steps_of(key, extent, pieces, low, high):
    gain, own = 1.0, jax.random.fold_in(key, 6)
    for dim, shards_of in pieces:
        steps = jnp.exp(jax.random.uniform(jax.random.fold_in(own, dim), (shards_of,), jnp.float32, low / len(pieces), high / len(pieces)))
        gain = gain * jnp.repeat(steps, extent[dim] // shards_of).reshape([-1 if axis == dim else 1 for axis in range(len(extent))])
    return gain


def noise(own_key, dims, deviation, reach, cuts=(), held_as=jnp.bfloat16):
    loudness = steps_of(own_key, dims, cuts, -0.22, 0.18) if cuts else 1.0
    entries = jax.random.normal(own_key, dims, jnp.float32) * deviation * loudness
    return jnp.minimum(jnp.maximum(entries, -reach), reach).astype(held_as)


def setup_inputs(seed: int = 0) -> dict:
    streams_of = jax.random.split(jax.random.key(seed), 12)
    return {
        "fields": noise(streams_of[0], (4, LEV, NLAT, NLON), 1.0, 6.0, ((2, 8), (3, 16)), jnp.float32),
        "courant_lon": jnp.clip(jax.random.uniform(streams_of[1], (LEV, NLAT, NLON), jnp.float32, -0.3, 0.3) * steps_of(streams_of[1], (LEV, NLAT, NLON), ((1, 8), (2, 16)), -0.4, 0.0), -0.3, 0.3),
        "courant_lat": jnp.clip(jax.random.uniform(streams_of[2], (LEV, NLAT, NLON), jnp.float32, -0.3, 0.3) * steps_of(streams_of[2], (LEV, NLAT, NLON), ((1, 8), (2, 16)), -0.4, 0.0), -0.3, 0.3),
        "diffusion": jnp.clip(0.1 + 0.13999999 * jax.random.uniform(streams_of[3], (LEV, NLAT, NLON), jnp.float32) ** steps_of(streams_of[3], (LEV, NLAT, NLON), ((1, 8), (2, 16)), -0.2, 0.2), 0.1, 0.24),
        "tend_cot": noise(streams_of[4], (4, LEV, NLAT, NLON), 1.0, 6.0, ((2, 8), (3, 16))),
        "col_list": draw_col_list(jax.random.fold_in(streams_of[11], 71), 0),
        "block_count": draw_block_count(jax.random.fold_in(streams_of[11], 71), 0),
        "block_dest": jax.vmap(lambda own: jax.random.permutation(own, N_LON))(jax.random.split(streams_of[7], N_LAT * N_LON)).reshape((N_LAT, N_LON, N_LON)).astype(jnp.int32),
        "w_in": noise(streams_of[8], (EXPERTS, FEAT, HID), FEAT ** -0.5, 0.3125, ((0, 16), (2, 8))),
        "w_mid": noise(streams_of[9], (EXPERTS, HID, HID), HID ** -0.5, 0.25, ((0, 16), (2, 8))),
        "w_out": noise(streams_of[10], (EXPERTS, FEAT, HID), HID ** -0.5, 0.25, ((0, 16), (2, 8))),
    }


def dsilu(value):
    sig = jax.nn.sigmoid(value)
    return sig * (1.0 + value * (1.0 - sig))

def physics(x, g, weights, shared):
    w_first, w_second, w_third = weights
    lead = 'e' if shared else 'b'
    xf = x.astype(jnp.float32)
    scale = lax.rsqrt(lax.optimization_barrier(jnp.mean(xf * xf, axis=0, keepdims=True)) + 1e-06)
    xn = (xf * scale).astype(jnp.bfloat16)
    a_one = jnp.einsum(lead + 'fh,fbc->hbc', w_first, xn, preferred_element_type=jnp.float32)
    h_one = jax.nn.silu(a_one).astype(jnp.bfloat16)
    a_two = jnp.einsum(lead + 'gh,gbc->hbc', w_second, h_one, preferred_element_type=jnp.float32)
    h_two = jax.nn.silu(a_two).astype(jnp.bfloat16)
    tend = jnp.einsum(lead + 'fh,hbc->fbc', w_third, h_two, preferred_element_type=jnp.float32).astype(jnp.bfloat16)
    back_two = jnp.einsum(lead + 'fh,fbc->hbc', w_third, g, preferred_element_type=jnp.float32)
    d_two = (back_two * dsilu(a_two)).astype(jnp.bfloat16)
    back_one = jnp.einsum(lead + 'gh,hbc->gbc', w_second, d_two, preferred_element_type=jnp.float32)
    d_one = (back_one * dsilu(a_one)).astype(jnp.bfloat16)
    d_norm = jnp.einsum(lead + 'fh,hbc->fbc', w_first, d_one, preferred_element_type=jnp.float32)
    adj = (scale * d_norm - xf * (scale * scale * scale) * lax.optimization_barrier(jnp.mean(xf * d_norm, axis=0, keepdims=True))).astype(jnp.bfloat16)
    out_form = 'fh' if shared else 'bfh'
    mid_form = 'gh' if shared else 'bgh'
    grad_first = jnp.einsum('fbc,hbc->' + out_form, xn, d_one, preferred_element_type=jnp.float32)
    grad_second = jnp.einsum('gbc,hbc->' + mid_form, h_one, d_two, preferred_element_type=jnp.float32)
    grad_third = jnp.einsum('fbc,hbc->' + out_form, g, h_two, preferred_element_type=jnp.float32)
    return (tend, adj, (grad_first, grad_second, grad_third))

def reference(fields, courant_lon, courant_lat, diffusion, tend_cot, col_list, block_count, block_dest, w_in, w_mid, w_out):
    state = fields
    for step in range(STEPS):
        east = jnp.roll(state, -1, axis=3)
        west = jnp.roll(state, 1, axis=3)
        padded = jnp.pad(state, ((0, 0), (0, 0), (1, 1), (0, 0)))
        north = padded[:, :, 2:]
        south = padded[:, :, :-2]
        state = state - 0.5 * courant_lon * (east - west) - 0.5 * courant_lat * (north - south) + diffusion * (east + west + north + south - 4.0 * state)
    feat = 4 * LEV
    ncol = CLAT * CLON
    devs = N_LAT * N_LON

    def tiles(array):
        return array.reshape(4, LEV, N_LAT, CLAT, N_LON, CLON).transpose(2, 4, 0, 1, 3, 5).reshape(N_LAT, N_LON, feat, ncol)

    def untile(array):
        return array.reshape(N_LAT, N_LON, 4, LEV, CLAT, CLON).transpose(2, 3, 0, 4, 1, 5).reshape(4, LEV, N_LAT * CLAT, N_LON * CLON)
    col_tiles = tiles(fields.astype(jnp.bfloat16))
    cot_tiles = tiles(tend_cot)
    slot_table = col_list.reshape(N_LAT, N_LON, N_LON, BLK)

    def expert(index):
        pick = (block_dest == index).astype(jnp.int32)
        which = jnp.argmax(pick, axis=2).astype(jnp.int32)
        cols = jnp.take_along_axis(slot_table, which[:, :, None, None], axis=2)[:, :, 0]
        count = jnp.take_along_axis(block_count, which[:, :, None], axis=2)[:, :, 0]
        live = jnp.arange(BLK, dtype=jnp.int32)[None, None, :] < count[:, :, None]
        xs = jnp.take_along_axis(col_tiles, cols[:, :, None, :], axis=3)
        gs = jnp.take_along_axis(cot_tiles, cols[:, :, None, :], axis=3)
        xs = jnp.where(live[:, :, None, :], xs, jnp.zeros_like(xs))
        gs = jnp.where(live[:, :, None, :], gs, jnp.zeros_like(gs))
        x_block = xs.reshape(devs, feat, BLK).transpose(1, 0, 2)
        g_block = gs.reshape(devs, feat, BLK).transpose(1, 0, 2)
        weights = (w_in[index][None], w_mid[index][None], w_out[index][None])
        tend, adj, grads = physics(x_block, g_block, weights, True)
        return (tend, adj, cols.reshape(devs, BLK), grads[0], grads[1], grads[2])
    tends, adjs, cols_all, grad_in, grad_mid, grad_out = lax.map(expert, jnp.arange(N_LON, dtype=jnp.int32))
    dev_index = jnp.broadcast_to(jnp.arange(devs, dtype=jnp.int32)[None, :, None], cols_all.shape)
    tend_full = jnp.zeros((devs, feat, ncol), jnp.bfloat16).at[dev_index, :, cols_all].set(tends.transpose(0, 2, 3, 1))
    adj_full = jnp.zeros((devs, feat, ncol), jnp.bfloat16).at[dev_index, :, cols_all].set(adjs.transpose(0, 2, 3, 1))
    new_fields = state + untile(tend_full).astype(jnp.float32)
    adjoint = untile(adj_full)
    return (new_fields, adjoint, grad_in, grad_mid, grad_out)
```

```python
import jax
import jax.numpy as jnp
from jax import lax
from jax.experimental import pallas as pl
from jax.experimental.pallas import tpu as pltpu
from jax.sharding import PartitionSpec as P


STEPS = 4
LANE = 128
WIDE = 4
GROUP = 32
LEVELS = 16
F32 = jnp.float32
BF16 = jnp.bfloat16


def iota(shape, dim):
    return lax.broadcasted_iota(jnp.int32, shape, dim)


def rows_of_source(src_ref, mat_ref, rows):
    for r in range(rows):
        mat_ref[:, r * LANE : (r + 1) * LANE] = src_ref[pl.ds(r, mat_ref.shape[0], stride=rows), :].astype(BF16)


def gather_blocks(table_ref, mat_ref, out_ref):
    ncol = mat_ref.shape[1]
    first = pl.program_id(0) * WIDE
    column = iota((ncol, LANE), 0)
    hot = [jnp.where(column == table_ref[pl.ds(first + b, 1), :], 1.0, 0.0).astype(BF16) for b in range(WIDE)]
    got = jnp.dot(mat_ref[...], jnp.concatenate(hot, axis=1), preferred_element_type=F32).astype(BF16)
    for b in range(WIDE):
        out_ref[b] = got[:, b * LANE : (b + 1) * LANE]


def gather_first_kernel(dest_ref, count_ref, cols_ref, src_ref, out_ref, table_ref, mat_ref, *, rows):
    @pl.when(pl.program_id(0) == 0)
    def _():
        slot = iota((1, LANE), 1)
        for b in range(cols_ref.shape[0]):
            row = jnp.where(slot < count_ref[0, 0, b], cols_ref[b], -1)
            table_ref[pl.ds(dest_ref[0, 0, b], 1), :] = row
        rows_of_source(src_ref, mat_ref, rows)

    gather_blocks(table_ref, mat_ref, out_ref)


def gather_kernel(table_ref, src_ref, out_ref, mat_ref, wide_ref, *, rows):
    @pl.when(pl.program_id(0) == 0)
    def _():
        wide_ref[...] = src_ref[...].astype(F32)
        rows_of_source(wide_ref, mat_ref, rows)

    gather_blocks(table_ref, mat_ref, out_ref)


def gather_parts(source, nblock, feat, rows):
    once = pl.BlockSpec(source.shape, lambda i: (0, 0), pipeline_mode=pl.Buffered(1))
    out = pl.BlockSpec((WIDE, feat, LANE), lambda i: (i, 0, 0))
    shape = jax.ShapeDtypeStruct((nblock, feat, LANE), BF16)
    cost = pl.CostEstimate(
        flops=2 * feat * rows * LANE * nblock * LANE,
        transcendentals=0,
        bytes_accessed=source.size * source.dtype.itemsize + feat * nblock * LANE * 2,
    )
    return once, out, shape, cost


def gather_first(dest, count, cols, source, feat, rows):
    nblock = cols.shape[0]
    once, out, shape, cost = gather_parts(source, nblock, feat, rows)
    table = jax.ShapeDtypeStruct((nblock, LANE), jnp.int32)

    def kernel(*refs):
        gather_first_kernel(*refs, rows=rows)

    scalars = pl.BlockSpec(memory_space=pltpu.SMEM)
    return pl.pallas_call(
        kernel,
        grid=(nblock // WIDE,),
        in_specs=[scalars, scalars, pl.BlockSpec(cols.shape, lambda i: (0, 0, 0)), once],
        out_specs=[out, pl.BlockSpec(table.shape, lambda i: (0, 0))],
        out_shape=[shape, table],
        scratch_shapes=[pltpu.VMEM((feat, rows * LANE), BF16)],
        cost_estimate=cost,
        name="gather_first",
    )(dest, count, cols, source)


def gather_columns(table, source, feat, rows):
    nblock = table.shape[0]
    once, out, shape, cost = gather_parts(source, nblock, feat, rows)

    def kernel(*refs):
        gather_kernel(*refs, rows=rows)

    return pl.pallas_call(
        kernel,
        grid=(nblock // WIDE,),
        in_specs=[pl.BlockSpec(table.shape, lambda i: (0, 0)), once],
        out_specs=out,
        out_shape=shape,
        scratch_shapes=[pltpu.VMEM((feat, rows * LANE), BF16), pltpu.VMEM(source.shape, F32)],
        cost_estimate=cost,
        name="gather_columns",
    )(table, source)


def scatter_rows(table_ref, blocks_ref, mat_ref, where_ref):
    nblock = blocks_ref.shape[0]

    @pl.when(pl.program_id(0) == 0)
    def _():
        table = table_ref[...].astype(F32)
        by_slot = jnp.concatenate([table, jnp.zeros((LANE - nblock, LANE), F32)], axis=0).T
        for b in range(nblock):
            mat_ref[:, b * LANE : (b + 1) * LANE] = blocks_ref[b]
            column = jnp.broadcast_to(by_slot[:, b : b + 1], (LANE, LANE))
            where_ref[b * LANE : (b + 1) * LANE, :] = column.astype(jnp.int32)

    where = where_ref[...]
    lane = iota(where.shape, 1) + pl.program_id(0) * (WIDE * LANE)
    hot = [jnp.where(where == lane + r * LANE, 1.0, 0.0).astype(BF16) for r in range(WIDE)]
    return jnp.dot(mat_ref[...], jnp.concatenate(hot, axis=1), preferred_element_type=F32)


def scatter_add_kernel(table_ref, blocks_ref, base_ref, out_ref, mat_ref, where_ref, *, rows):
    got = scatter_rows(table_ref, blocks_ref, mat_ref, where_ref)
    for r in range(WIDE):
        at = pl.ds(pl.program_id(0) * WIDE + r, mat_ref.shape[0], stride=rows)
        out_ref[at, :] = base_ref[at, :] + got[:, r * LANE : (r + 1) * LANE]


def scatter_kernel(table_ref, blocks_ref, out_ref, mat_ref, where_ref, full_ref, *, rows):
    got = scatter_rows(table_ref, blocks_ref, mat_ref, where_ref)
    for r in range(WIDE):
        at = pl.ds(pl.program_id(0) * WIDE + r, mat_ref.shape[0], stride=rows)
        full_ref[at, :] = got[:, r * LANE : (r + 1) * LANE]

    @pl.when(pl.program_id(0) == pl.num_programs(0) - 1)
    def _():
        out_ref[...] = full_ref[...].astype(BF16)


def scatter_columns(table, blocks, rows, base=None):
    nblock, feat, length = blocks.shape
    nslot = nblock * length
    shape = (feat * rows, LANE)
    whole = pl.BlockSpec(shape, lambda i: (0, 0), pipeline_mode=pl.Buffered(1))
    specs = [
        pl.BlockSpec(table.shape, lambda i: (0, 0)),
        pl.BlockSpec(blocks.shape, lambda i: (0, 0, 0), pipeline_mode=pl.Buffered(1)),
    ]
    scratch = [pltpu.VMEM((feat, nslot), BF16), pltpu.VMEM((nslot, LANE), jnp.int32)]
    if base is None:
        body, operands, dtype = scatter_kernel, (table, blocks), BF16
        scratch.append(pltpu.VMEM(shape, F32))
    else:
        body, operands, dtype = scatter_add_kernel, (table, blocks, base), F32
        specs.append(whole)

    def kernel(*refs):
        body(*refs, rows=rows)

    return pl.pallas_call(
        kernel,
        grid=(rows // WIDE,),
        in_specs=specs,
        out_specs=pl.BlockSpec(shape, lambda i: (0, 0)),
        out_shape=jax.ShapeDtypeStruct(shape, dtype),
        scratch_shapes=scratch,
        cost_estimate=pl.CostEstimate(
            flops=2 * feat * nslot * rows * LANE, transcendentals=0, bytes_accessed=feat * nslot * 8
        ),
        name="scatter_columns",
    )(*operands)


def wide(ref):
    return jnp.concatenate([ref[b] for b in range(ref.shape[0])], axis=1)


def normalised(x):
    xf = x.astype(F32)
    scale = lax.rsqrt(jnp.mean(xf * xf, axis=0, keepdims=True) + 1e-06)
    return xf, scale, (xf * scale).astype(BF16)


def mul(a, b):
    return jnp.dot(a, b, preferred_element_type=F32)


def mul_slots(a, b):
    return lax.dot_general(a, b, (((1,), (1,)), ((), ())), preferred_element_type=F32)


def forward_kernel(x_ref, wt_ref, w_ref, tend_ref, a1_ref, a2_ref, *, cuts):
    (in0, in1), (mid0, mid1), (out0, out1) = cuts
    _, _, xn = normalised(wide(x_ref))
    a_one = mul(wt_ref[:, in0:in1], xn)
    a1_ref[...] = a_one
    h_one = (a_one * jax.nn.sigmoid(a_one)).astype(BF16)
    a_two = mul(wt_ref[:, mid0:mid1], h_one)
    a2_ref[...] = a_two
    h_two = (a_two * jax.nn.sigmoid(a_two)).astype(BF16)
    tend = mul(w_ref[out0:out1, :], h_two).astype(BF16)
    for b in range(x_ref.shape[0]):
        tend_ref[b] = tend[:, b * LANE : (b + 1) * LANE]


def backward_kernel(x_ref, g_ref, a1_ref, a2_ref, wt_ref, w_ref, adj_ref, grad_ref, sum_ref, *, cuts):
    (in0, in1), (mid0, mid1), (out0, out1) = cuts

    @pl.when(pl.program_id(0) == 0)
    def _():
        sum_ref[...] = jnp.zeros_like(sum_ref)

    xf, scale, xn = normalised(wide(x_ref))
    g = wide(g_ref)
    a_two = a2_ref[...]
    sig = jax.nn.sigmoid(a_two)
    h_two = (a_two * sig).astype(BF16)
    d_two = (mul(wt_ref[:, out0:out1], g) * (sig * (1.0 + a_two * (1.0 - sig)))).astype(BF16)
    sum_ref[:, out0:out1] += mul_slots(h_two, g)
    a_one = a1_ref[...]
    sig = jax.nn.sigmoid(a_one)
    h_one = (a_one * sig).astype(BF16)
    d_one = (mul(w_ref[mid0:mid1, :], d_two) * (sig * (1.0 + a_one * (1.0 - sig)))).astype(BF16)
    sum_ref[:, mid0:mid1] += mul_slots(d_two, h_one)
    d_norm = mul(w_ref[in0:in1, :], d_one)
    adj = (
        scale * d_norm - xf * (scale * scale * scale) * jnp.mean(xf * d_norm, axis=0, keepdims=True)
    ).astype(BF16)
    for b in range(x_ref.shape[0]):
        adj_ref[b] = adj[:, b * LANE : (b + 1) * LANE]
    sum_ref[:, in0:in1] += mul_slots(d_one, xn)

    @pl.when(pl.program_id(0) == pl.num_programs(0) - 1)
    def _():
        grad_ref[...] = sum_ref[...].astype(BF16)


def column_specs(shape, pair, hid, span):
    _, feat, length = shape
    block = pl.BlockSpec((pair, feat, length), lambda i: (i, 0, 0))
    hidden = pl.BlockSpec((hid, pair * length), lambda i: (0, i))
    w_t = pl.BlockSpec((hid, span), lambda i: (0, 0), pipeline_mode=pl.Buffered(1))
    w = pl.BlockSpec((span, hid), lambda i: (0, 0), pipeline_mode=pl.Buffered(1))
    return block, hidden, w_t, w


def physics_forward(x, w_t, w, cuts):
    nblock, feat, length = x.shape
    hid, span = w_t.shape
    pair = WIDE
    block, hidden, spec_t, spec = column_specs(x.shape, pair, hid, span)

    def kernel(*refs):
        forward_kernel(*refs, cuts=cuts)

    kept = jax.ShapeDtypeStruct((hid, nblock * length), F32)
    return pl.pallas_call(
        kernel,
        grid=(nblock // pair,),
        in_specs=[block, spec_t, spec],
        out_specs=[block, hidden, hidden],
        out_shape=[jax.ShapeDtypeStruct(x.shape, BF16), kept, kept],
        cost_estimate=pl.CostEstimate(
            flops=2 * hid * (2 * feat + hid) * nblock * length,
            transcendentals=4 * hid * nblock * length,
            bytes_accessed=x.size * 4 + hid * nblock * length * 8,
        ),
        name="physics_forward",
    )(x, w_t, w)


def physics_backward(x, g, a_one, a_two, w_t, w, cuts):
    nblock, feat, length = x.shape
    hid, span = w_t.shape
    pair = WIDE
    block, hidden, spec_t, spec = column_specs(x.shape, pair, hid, span)

    def kernel(*refs):
        backward_kernel(*refs, cuts=cuts)

    return pl.pallas_call(
        kernel,
        grid=(nblock // pair,),
        in_specs=[block, block, hidden, hidden, spec_t, spec],
        out_specs=[block, pl.BlockSpec((hid, span), lambda i: (0, 0))],
        out_shape=[jax.ShapeDtypeStruct(x.shape, BF16), jax.ShapeDtypeStruct((hid, span), BF16)],
        scratch_shapes=[pltpu.VMEM((hid, span), F32)],
        cost_estimate=pl.CostEstimate(
            flops=4 * hid * (2 * feat + hid) * nblock * length,
            transcendentals=4 * hid * nblock * length,
            bytes_accessed=x.size * 6 + hid * nblock * length * 8,
        ),
        name="physics_backward",
    )(x, g, a_one, a_two, w_t, w)


def plane(fields_ref, coef_refs, a, at):
    nfield = fields_ref.shape[0]
    return fields_ref[a, at, :] if a < nfield else coef_refs[a - nfield][at, :]


def inside(levels):
    return iota((GROUP, LANE), 0) + pl.program_id(0) * GROUP < levels


def rim_kernel(fields_ref, lon_ref, lat_ref, dif_ref, low_ref, high_ref, *, rows, levels):
    coefs = (lon_ref, lat_ref, dif_ref)
    keep = inside(levels)
    for r in range(STEPS):
        for a in range(low_ref.shape[1]):
            for first, out in ((r, low_ref), (rows - STEPS + r, high_ref)):
                value = plane(fields_ref, coefs, a, pl.ds(first, GROUP, stride=rows))
                out[r, a] = jnp.where(keep, value, 0.0).astype(BF16)


def strip_kernel(
    fields_ref, lon_ref, lat_ref, dif_ref, south_ref, north_ref, west_ref, east_ref, all_ref, sum_ref, *, rows, levels
):
    coefs = (lon_ref, lat_ref, dif_ref)
    planes = south_ref.shape[1]
    keep = inside(levels)
    for t in range(rows + 2 * STEPS):
        for a in range(planes):
            if t < STEPS:
                value = south_ref[t, a]
            elif t >= rows + STEPS:
                value = north_ref[t - rows - STEPS, a]
            else:
                own = plane(fields_ref, coefs, a, pl.ds(t - STEPS, GROUP, stride=rows))
                value = jnp.where(keep, own, 0.0).astype(BF16)
            all_ref[t * GROUP : (t + 1) * GROUP, a * LANE : (a + 1) * LANE] = value
    shape = (planes * LANE, 2 * LANE)
    k, n = iota(shape, 0), iota(shape, 1)
    a, q = k // LANE, k % LANE
    west = jnp.where(q < STEPS, STEPS * a + q, -1)
    east = jnp.where(q >= LANE - STEPS, STEPS * a + q - (LANE - STEPS) + LANE, -1)
    pick = jnp.where((n == west) | (n == east), 1.0, 0.0).astype(BF16)
    got = jnp.dot(all_ref[...], pick, preferred_element_type=F32)
    group = pl.program_id(0)

    @pl.when(group == 0)
    def _():
        sum_ref[...] = got

    @pl.when(group > 0)
    def _():
        for half in range(2):
            part = got[:, half * LANE : (half + 1) * LANE]
            sum_ref[:, half * LANE : (half + 1) * LANE] += pltpu.roll(part, group * GROUP, 1)

    @pl.when(group == pl.num_programs(0) - 1)
    def _():
        west_ref[...] = sum_ref[:, :LANE].astype(BF16)
        east_ref[...] = sum_ref[:, LANE:].astype(BF16)


def weights_of(c_lon, c_lat, c_dif):
    return (
        1.0 - 4.0 * c_dif,
        c_dif - 0.5 * c_lon,
        c_dif + 0.5 * c_lon,
        c_dif - 0.5 * c_lat,
        c_dif + 0.5 * c_lat,
    )


def stepped(coef, centre, east, west, north, south):
    return coef[0] * centre + (coef[1] * east + coef[2] * west) + (coef[3] * north + coef[4] * south)


def dynamics_kernel(
    fields_ref,
    lon_ref,
    lat_ref,
    dif_ref,
    south_ref,
    north_ref,
    own_w_ref,
    own_e_ref,
    from_e_ref,
    from_w_ref,
    out_ref,
    rim_ref,
    strip_ref,
    coef_ref,
    join_ref,
    state_ref,
    shift_ref,
    *,
    rows,
):
    coefs = (lon_ref, lat_ref, dif_ref)
    nfield = fields_ref.shape[0]
    total = rows + 2 * STEPS
    rim_ref[0] = south_ref[...].astype(F32)
    rim_ref[1] = north_ref[...].astype(F32)

    sources = jnp.concatenate([own_e_ref[...], from_e_ref[...], from_w_ref[...], own_w_ref[...]], axis=1)
    shape = (4 * LANE, 4 * LANE)
    k, n = iota(shape, 0), iota(shape, 1)
    lane, kind, m = k % LANE, n // LANE, n % LANE
    row_code = (k // LANE) * STEPS + lane % STEPS + 16 * ((lane // STEPS) % 8)
    row_code = jnp.where(lane // GROUP == pl.program_id(0), row_code, -1)
    col_code = jnp.where(kind == 0, m, m % 16 + 16 * (nfield - 1 + kind))
    col_code = jnp.where(m < 16 * nfield, col_code, -2)
    pick = jnp.where(row_code == col_code, 1.0, 0.0).astype(BF16)
    strip_ref[...] = jnp.dot(sources, pick, preferred_element_type=F32)

    @pl.when(pl.program_id(0) == 0)
    def _():
        shape = (2 * LANE, 2 * LANE)
        k, n = iota(shape, 0), iota(shape, 1)
        east = jnp.where(k < LANE, k - 1, jnp.where(k % 16 == 4, LANE - 1, -1))
        west = jnp.where(k < LANE - 1, k + 1 + LANE, jnp.where((k >= LANE) & (k % 16 == 11), LANE, -1))
        shift_ref[...] = jnp.where(((n == east) & (k > 0)) | (n == west), 1.0, 0.0).astype(BF16)

    part = LEVELS
    field_of_lane = iota((part, LANE), 1) // 16

    def levels(sub, carry):
        def cell(a, t):
            if STEPS <= t < rows + STEPS:
                return plane(fields_ref, coefs, a, pl.ds(sub * (part * rows) + t - STEPS, part, stride=rows))
            side, at = (0, t) if t < STEPS else (1, t - rows - STEPS)
            return rim_ref[side, at, a, pl.ds(sub * part, part), :]

        def strip(kind, t):
            return strip_ref[pl.ds(t * GROUP + sub * part, part), kind * LANE : (kind + 1) * LANE]

        for t in range(1, total - 1):
            at = slice(t * part, (t + 1) * part)
            for c, value in enumerate(weights_of(cell(nfield, t), cell(nfield + 1, t), cell(nfield + 2, t))):
                coef_ref[0, c, at] = value
            for c, value in enumerate(weights_of(strip(1, t), strip(2, t), strip(3, t))):
                coef_ref[1, c, at] = value
        for f in range(nfield):
            for t in range(total):
                state_ref[0, f, t * part : (t + 1) * part] = cell(f, t)

        state = {t: strip(0, t) for t in range(total)}
        for step in range(STEPS):
            inner = range(step + 1, total - 1 - step)
            for t in inner:
                for f in range(nfield):
                    join_ref[step, f, t * part : (t + 1) * part] = jnp.where(field_of_lane == f, state[t], 0.0).astype(BF16)
            if step < STEPS - 1:
                state = {
                    t: stepped(
                        [coef_ref[1, c, t * part : (t + 1) * part] for c in range(5)],
                        state[t],
                        pltpu.roll(state[t], LANE - 1, 1),
                        pltpu.roll(state[t], 1, 1),
                        state[t + 1],
                        state[t - 1],
                    )
                    for t in inner
                }

        def rows_of(step, by=0):
            return slice((step + 1 + by) * part, (total - 1 - step + by) * part)

        def neighbours(step, pair):
            at = rows_of(step)
            cells = [
                jnp.concatenate([state_ref[step % 2, f, at].astype(BF16), join_ref[step, f, at]], axis=1) for f in pair
            ]
            return mul(jnp.concatenate(cells, axis=0), shift_ref[...])

        turns = [(step, pair) for step in range(STEPS) for pair in ((0, 1), (2, 3))]
        ready = neighbours(*turns[0])
        for turn, (step, pair) in enumerate(turns):
            sides = ready
            if turn + 1 < len(turns):
                ready = neighbours(*turns[turn + 1])
            size = (total - 2 - 2 * step) * part
            coef = [coef_ref[0, c, rows_of(step)] for c in range(5)]
            for n, f in enumerate(pair):
                cur = step % 2
                value = stepped(
                    coef,
                    state_ref[cur, f, rows_of(step)],
                    sides[n * size : (n + 1) * size, :LANE],
                    sides[n * size : (n + 1) * size, LANE:],
                    state_ref[cur, f, rows_of(step, 1)],
                    state_ref[cur, f, rows_of(step, -1)],
                )
                if step < STEPS - 1:
                    state_ref[1 - cur, f, rows_of(step)] = value
                    continue
                for r in range(rows):
                    out_ref[f, pl.ds(sub * (part * rows) + r, part, stride=rows), :] = value[r * part : (r + 1) * part]
        return carry

    lax.fori_loop(0, GROUP // part, levels, 0)


class Dynamics:
    def __init__(self, fields, coefs, rows, levels):
        self.args = (fields, *coefs)
        self.rows, self.levels = rows, levels
        nfield = fields.shape[0]
        planes = nfield + len(coefs)
        groups = pl.cdiv(levels, GROUP)
        self.grid = (groups,)
        self.planes = planes
        self.strip_rows = (rows + 2 * STEPS) * GROUP
        self.fields_spec = pl.BlockSpec((nfield, GROUP * rows, LANE), lambda i: (0, i, 0))
        self.arg_specs = [self.fields_spec] + [pl.BlockSpec((GROUP * rows, LANE), lambda i: (i, 0))] * 3
        self.rim_spec = pl.BlockSpec((STEPS, planes, GROUP, LANE), lambda i: (0, 0, i, 0))
        self.rim_shape = jax.ShapeDtypeStruct((STEPS, planes, groups * GROUP, LANE), BF16)
        self.strip_spec = pl.BlockSpec((self.strip_rows, LANE), lambda i: (0, 0))
        self.strip_shape = jax.ShapeDtypeStruct((self.strip_rows, LANE), BF16)

    def rims(self):
        def kernel(*refs):
            rim_kernel(*refs, rows=self.rows, levels=self.levels)

        return pl.pallas_call(
            kernel,
            grid=self.grid,
            in_specs=self.arg_specs,
            out_specs=[self.rim_spec, self.rim_spec],
            out_shape=[self.rim_shape, self.rim_shape],
            name="rims",
        )(*self.args)

    def send_rims(self, low, high):
        size = lax.axis_size("lat")
        up = [(i, i + 1) for i in range(size - 1)]
        south = lax.ppermute(high, "lat", up)
        north = lax.ppermute(low, "lat", [(j, i) for i, j in up])
        return south, north

    def strips(self, south, north, start):
        def kernel(*refs):
            strip_kernel(*refs, rows=self.rows, levels=self.levels)

        south, north = after((south, north), start)
        return pl.pallas_call(
            kernel,
            grid=self.grid,
            in_specs=self.arg_specs + [self.rim_spec, self.rim_spec],
            out_specs=[self.strip_spec, self.strip_spec],
            out_shape=[self.strip_shape, self.strip_shape],
            scratch_shapes=[
                pltpu.VMEM((self.strip_rows, self.planes * LANE), BF16),
                pltpu.VMEM((self.strip_rows, 2 * LANE), F32),
            ],
            name="strips",
        )(*self.args, south, north)

    def send_strips(self, own_w, own_e):
        size = lax.axis_size("lon")
        around = [(i, (i + 1) % size) for i in range(size)]
        from_w = lax.ppermute(own_e, "lon", around)
        from_e = lax.ppermute(own_w, "lon", [(j, i) for i, j in around])
        return from_w, from_e

    def steps(self, south, north, own_w, own_e, from_w, from_e, start):
        def kernel(*refs):
            dynamics_kernel(*refs, rows=self.rows)

        fields = self.args[0]
        from_w, from_e = after((from_w, from_e), start)
        return pl.pallas_call(
            kernel,
            grid=self.grid,
            in_specs=self.arg_specs + [self.rim_spec, self.rim_spec] + [self.strip_spec] * 4,
            out_specs=self.fields_spec,
            out_shape=jax.ShapeDtypeStruct(fields.shape, F32),
            scratch_shapes=[
                pltpu.VMEM((2, STEPS, self.planes, GROUP, LANE), F32),
                pltpu.VMEM((self.strip_rows, 4 * LANE), F32),
                pltpu.VMEM((2, 5, (self.rows + 2 * STEPS) * LEVELS, LANE), F32),
                pltpu.VMEM((STEPS, fields.shape[0], (self.rows + 2 * STEPS) * LEVELS, LANE), BF16),
                pltpu.VMEM((2, fields.shape[0], (self.rows + 2 * STEPS) * LEVELS, LANE), F32),
                pltpu.VMEM((2 * LANE, 2 * LANE), BF16),
            ],
            cost_estimate=pl.CostEstimate(flops=fields.size * 60, transcendentals=0, bytes_accessed=fields.size * 11),
            name="dynamics",
        )(*self.args, south, north, own_w, own_e, from_e, from_w)


def after(values, start):
    return lax.optimization_barrier((values, start))[0]


def exchange(array, axis):
    return lax.all_to_all(array, axis, split_axis=0, concat_axis=0, tiled=True)


def scattered(parts):
    size = parts.shape[0]
    core = lax.axis_index("lat") % 2
    pairs = parts.reshape((size // 2, 2) + parts.shape[1:])
    mine = lax.dynamic_index_in_dim(pairs, core, 1, keepdims=False)
    other = lax.dynamic_index_in_dim(pairs, 1 - core, 1, keepdims=False)
    other = lax.ppermute(other, "lat", [(i, i ^ 1) for i in range(size)])
    both = mine.astype(F32) + other.astype(F32)
    chips = size // 2
    chip = lax.axis_index("lat") // 2
    total = lax.dynamic_index_in_dim(both, chip, 0, keepdims=False)
    both = both.astype(BF16)
    for shift in range(1, chips):
        part = lax.dynamic_index_in_dim(both, (chip + shift) % chips, 0, keepdims=False)
        to = [(i, (i + 2 * shift) % size) for i in range(size)]
        total = total + lax.ppermute(part, "lat", to).astype(F32)
    return total


def shards(
    fields,
    courant_lon,
    courant_lat,
    diffusion,
    tend_cot,
    col_list,
    block_count,
    block_dest,
    w_in,
    w_mid,
    w_out,
):
    nfield, levels, rows, columns = fields.shape
    feat = nfield * levels
    hid_mid, hid_own = w_mid.shape[1:]
    nlat = lax.axis_size("lat")
    pad = -feat % LANE
    cuts = (
        (0, feat),
        (feat + pad, feat + pad + hid_mid),
        (feat + pad + hid_mid, 2 * feat + pad + hid_mid),
    )
    span = cuts[2][1] + pad

    rest = jnp.zeros((pad, hid_own), BF16)
    own = jnp.concatenate([w_in[0], rest, w_mid[0], w_out[0], rest], axis=0).T
    w_t = exchange(jnp.broadcast_to(own[None], (nlat,) + own.shape), "lat").reshape(nlat * hid_own, span)
    w = w_t.T
    coefs = [c.reshape(levels * rows, columns) for c in (courant_lon, courant_lat, diffusion)]
    window = Dynamics(fields.reshape(nfield, levels * rows, columns), coefs, rows, levels)

    nblock = block_dest.shape[-1]
    low, high = window.rims()
    south, north = window.send_rims(low, high)
    cols = after(col_list.reshape(nblock, 1, LANE), low)
    send_x, table = gather_first(block_dest, block_count, cols, fields.reshape(feat * rows, columns), feat, rows)
    recv_x = exchange(send_x, "lon")
    own_w, own_e = window.strips(south, north, send_x)
    send_g = gather_columns(after(table, own_w), tend_cot.reshape(feat * rows, columns), feat, rows)
    recv_g = exchange(send_g, "lon")
    from_w, from_e = window.send_strips(own_w, own_e)
    tend, a_one, a_two = physics_forward(after(recv_x, send_g), w_t, w, cuts)
    back_tend = exchange(tend, "lon")
    state = window.steps(south, north, own_w, own_e, from_w, from_e, tend)
    adj, grads = physics_backward(recv_x, after(recv_g, state), a_one, a_two, w_t, w, cuts)
    back_adj = exchange(after(adj, back_tend), "lon")
    summed = scattered(grads.reshape(nlat, hid_own, span)).T
    grad_in, grad_mid, grad_out = (summed[a:b][None] for a, b in cuts)

    new_fields = scatter_columns(table, back_tend, rows, state.reshape(feat * rows, columns))
    adjoint = scatter_columns(table, back_adj, rows)
    return (new_fields.reshape(fields.shape), adjoint.reshape(fields.shape), grad_in, grad_mid, grad_out)


def solution(mesh):
    return jax.shard_map(
        shards,
        mesh=mesh,
        in_specs=(
            P(None, None, "lat", "lon"),
            P(None, "lat", "lon"),
            P(None, "lat", "lon"),
            P(None, "lat", "lon"),
            P(None, None, "lat", "lon"),
            P("lat", "lon", None),
            P("lat", "lon", None),
            P("lat", "lon", None),
            P("lon", None, "lat"),
            P("lon", None, "lat"),
            P("lon", None, "lat"),
        ),
        out_specs=(
            P(None, None, "lat", "lon"),
            P(None, None, "lat", "lon"),
            P("lon", None, "lat"),
            P("lon", None, "lat"),
            P("lon", None, "lat"),
        ),
        check_vma=False,
    )
```

```python
import jax
import jax.numpy as jnp
from jax import lax
from jax.experimental import pallas as pl
from jax.experimental.pallas import tpu as pltpu
from jax.sharding import PartitionSpec as P


STEPS = 4
LANE = 128
WIDE = 4
GROUP = 32
LEVELS = 16
F32 = jnp.float32
BF16 = jnp.bfloat16


def iota(shape, dim):
    return lax.broadcasted_iota(jnp.int32, shape, dim)


def rows_of_source(src_ref, mat_ref, rows):
    for r in range(rows):
        mat_ref[:, r * LANE : (r + 1) * LANE] = src_ref[pl.ds(r, mat_ref.shape[0], stride=rows), :].astype(BF16)


def gather_blocks(table_ref, mat_ref, out_ref):
    ncol = mat_ref.shape[1]
    first = pl.program_id(0) * WIDE
    column = iota((ncol, LANE), 0)
    hot = [jnp.where(column == table_ref[pl.ds(first + b, 1), :], 1.0, 0.0).astype(BF16) for b in range(WIDE)]
    got = jnp.dot(mat_ref[...], jnp.concatenate(hot, axis=1), preferred_element_type=F32).astype(BF16)
    for b in range(WIDE):
        out_ref[b] = got[:, b * LANE : (b + 1) * LANE]


def gather_first_kernel(dest_ref, count_ref, cols_ref, src_ref, out_ref, table_ref, mat_ref, full_ref, sems, *, rows):
    feat = mat_ref.shape[0]

    @pl.when(pl.program_id(0) == 0)
    def _():
        cuts = [(start, min(start + LANE, feat)) for start in range(0, feat, LANE)]
        loads = []
        for n, (start, stop) in enumerate(cuts):
            at = pl.ds(start * rows, (stop - start) * rows)
            loads.append(pltpu.make_async_copy(src_ref.at[at], full_ref.at[at], sems.at[n]))
            loads[-1].start()
        slot = iota((1, LANE), 1)
        for b in range(cols_ref.shape[0]):
            row = jnp.where(slot < count_ref[0, 0, b], cols_ref[b], -1)
            table_ref[pl.ds(dest_ref[0, 0, b], 1), :] = row
        for load, (start, stop) in zip(loads, cuts):
            load.wait()
            for r in range(rows):
                part = full_ref[pl.ds(start * rows + r, stop - start, stride=rows), :]
                mat_ref[start:stop, r * LANE : (r + 1) * LANE] = part.astype(BF16)

    gather_blocks(table_ref, mat_ref, out_ref)


def gather_kernel(table_ref, src_ref, out_ref, mat_ref, wide_ref, *, rows):
    @pl.when(pl.program_id(0) == 0)
    def _():
        wide_ref[...] = src_ref[...].astype(F32)
        rows_of_source(wide_ref, mat_ref, rows)

    gather_blocks(table_ref, mat_ref, out_ref)


def gather_parts(source, nblock, feat, rows):
    once = pl.BlockSpec(source.shape, lambda i: (0, 0), pipeline_mode=pl.Buffered(1))
    out = pl.BlockSpec((WIDE, feat, LANE), lambda i: (i, 0, 0))
    shape = jax.ShapeDtypeStruct((nblock, feat, LANE), BF16)
    cost = pl.CostEstimate(
        flops=2 * feat * rows * LANE * nblock * LANE,
        transcendentals=0,
        bytes_accessed=source.size * source.dtype.itemsize + feat * nblock * LANE * 2,
    )
    return once, out, shape, cost


def gather_first(dest, count, cols, source, feat, rows):
    nblock = cols.shape[0]
    _, out, shape, cost = gather_parts(source, nblock, feat, rows)
    table = jax.ShapeDtypeStruct((nblock, LANE), jnp.int32)

    def kernel(*refs):
        gather_first_kernel(*refs, rows=rows)

    scalars = pl.BlockSpec(memory_space=pltpu.SMEM)
    return pl.pallas_call(
        kernel,
        grid=(nblock // WIDE,),
        in_specs=[scalars, scalars, pl.BlockSpec(cols.shape, lambda i: (0, 0, 0)), pl.BlockSpec(memory_space=pl.ANY)],
        out_specs=[out, pl.BlockSpec(table.shape, lambda i: (0, 0))],
        out_shape=[shape, table],
        scratch_shapes=[
            pltpu.VMEM((feat, rows * LANE), BF16),
            pltpu.VMEM(source.shape, F32),
            pltpu.SemaphoreType.DMA((pl.cdiv(feat, LANE),)),
        ],
        cost_estimate=cost,
        name="gather_first",
    )(dest, count, cols, source)


def gather_columns(table, source, feat, rows):
    nblock = table.shape[0]
    once, out, shape, cost = gather_parts(source, nblock, feat, rows)

    def kernel(*refs):
        gather_kernel(*refs, rows=rows)

    return pl.pallas_call(
        kernel,
        grid=(nblock // WIDE,),
        in_specs=[pl.BlockSpec(table.shape, lambda i: (0, 0)), once],
        out_specs=out,
        out_shape=shape,
        scratch_shapes=[pltpu.VMEM((feat, rows * LANE), BF16), pltpu.VMEM(source.shape, F32)],
        cost_estimate=cost,
        name="gather_columns",
    )(table, source)


def scatter_rows(table_ref, blocks_ref, mat_ref, where_ref, sems):
    nblock = blocks_ref.shape[0]

    @pl.when(pl.program_id(0) == 0)
    def _():
        loads = []
        for b in range(nblock):
            to = mat_ref.at[:, pl.ds(b * LANE, LANE)]
            loads.append(pltpu.make_async_copy(blocks_ref.at[b], to, sems.at[b]))
            loads[-1].start()
        table = table_ref[...].astype(F32)
        by_slot = jnp.concatenate([table, jnp.zeros((LANE - nblock, LANE), F32)], axis=0).T
        for b in range(nblock):
            column = jnp.broadcast_to(by_slot[:, b : b + 1], (LANE, LANE))
            where_ref[b * LANE : (b + 1) * LANE, :] = column.astype(jnp.int32)
        for load in loads:
            load.wait()

    where = where_ref[...]
    lane = iota(where.shape, 1) + pl.program_id(0) * (WIDE * LANE)
    hot = [jnp.where(where == lane + r * LANE, 1.0, 0.0).astype(BF16) for r in range(WIDE)]
    return jnp.dot(mat_ref[...], jnp.concatenate(hot, axis=1), preferred_element_type=F32)


def scatter_add_kernel(table_ref, blocks_ref, base_ref, out_ref, mat_ref, where_ref, sems, full_ref, base_sem, *, rows):
    load = pltpu.make_async_copy(base_ref, full_ref, base_sem)

    @pl.when(pl.program_id(0) == 0)
    def _():
        load.start()

    got = scatter_rows(table_ref, blocks_ref, mat_ref, where_ref, sems)

    @pl.when(pl.program_id(0) == 0)
    def _():
        load.wait()

    for r in range(WIDE):
        at = pl.ds(pl.program_id(0) * WIDE + r, mat_ref.shape[0], stride=rows)
        out_ref[at, :] = full_ref[at, :] + got[:, r * LANE : (r + 1) * LANE]


def scatter_kernel(table_ref, blocks_ref, out_ref, mat_ref, where_ref, sems, full_ref, *, rows):
    got = scatter_rows(table_ref, blocks_ref, mat_ref, where_ref, sems)
    for r in range(WIDE):
        at = pl.ds(pl.program_id(0) * WIDE + r, mat_ref.shape[0], stride=rows)
        full_ref[at, :] = got[:, r * LANE : (r + 1) * LANE]

    @pl.when(pl.program_id(0) == pl.num_programs(0) - 1)
    def _():
        out_ref[...] = full_ref[...].astype(BF16)


def scatter_columns(table, blocks, rows, base=None):
    nblock, feat, length = blocks.shape
    nslot = nblock * length
    shape = (feat * rows, LANE)
    in_place = pl.BlockSpec(memory_space=pl.ANY)
    specs = [pl.BlockSpec(table.shape, lambda i: (0, 0)), in_place]
    scratch = [
        pltpu.VMEM((feat, nslot), BF16),
        pltpu.VMEM((nslot, LANE), jnp.int32),
        pltpu.SemaphoreType.DMA((nblock,)),
        pltpu.VMEM(shape, F32),
    ]
    if base is None:
        body, operands, dtype = scatter_kernel, (table, blocks), BF16
    else:
        body, operands, dtype = scatter_add_kernel, (table, blocks, base), F32
        specs.append(in_place)
        scratch.append(pltpu.SemaphoreType.DMA)

    def kernel(*refs):
        body(*refs, rows=rows)

    return pl.pallas_call(
        kernel,
        grid=(rows // WIDE,),
        in_specs=specs,
        out_specs=pl.BlockSpec(shape, lambda i: (0, 0)),
        out_shape=jax.ShapeDtypeStruct(shape, dtype),
        scratch_shapes=scratch,
        cost_estimate=pl.CostEstimate(
            flops=2 * feat * nslot * rows * LANE, transcendentals=0, bytes_accessed=feat * nslot * 8
        ),
        name="scatter_columns",
    )(*operands)


def wide(ref):
    return jnp.concatenate([ref[b] for b in range(ref.shape[0])], axis=1)


def normalised(x):
    xf = x.astype(F32)
    scale = lax.rsqrt(jnp.mean(xf * xf, axis=0, keepdims=True) + 1e-06)
    return xf, scale, (xf * scale).astype(BF16)


def mul(a, b):
    return jnp.dot(a, b, preferred_element_type=F32)


def mul_slots(a, b):
    return lax.dot_general(a, b, (((1,), (1,)), ((), ())), preferred_element_type=F32)


def place_weights(at_ref, piece_refs, w_t_ref, w_ref, parts):
    chips = len(piece_refs)
    size = piece_refs[0].shape[0] // 2
    for n, piece in enumerate(piece_refs):
        chip = (at_ref[0] + (chips - n)) % chips
        for half in range(2):
            core = at_ref[1] if half == 0 else 1 - at_ref[1]
            at = pl.multiple_of((2 * chip + core) * size, size)
            w_t_ref[pl.ds(at, size), :] = piece[half * size : (half + 1) * size, :]
    row = 0
    for start, stop in parts:
        w_ref[row : row + stop - start, :] = w_t_ref[:, start:stop].T
        row += stop - start


def forward_kernel(at_ref, x_ref, *refs, cuts):
    *piece_refs, tend_ref, a1_ref, a2_ref, w_t_ref, w_ref = refs
    (in0, in1), (mid0, mid1), (out0, out1) = cuts

    @pl.when(pl.program_id(0) == 0)
    def _():
        place_weights(at_ref, piece_refs, w_t_ref, w_ref, [(out0, w_t_ref.shape[1])])

    _, _, xn = normalised(wide(x_ref))
    a_one = mul(w_t_ref[:, in0:in1], xn)
    a1_ref[...] = a_one
    h_one = (a_one * jax.nn.sigmoid(a_one)).astype(BF16)
    a_two = mul(w_t_ref[:, mid0:mid1], h_one)
    a2_ref[...] = a_two
    h_two = (a_two * jax.nn.sigmoid(a_two)).astype(BF16)
    tend = mul(w_ref[: out1 - out0, :], h_two).astype(BF16)
    for b in range(x_ref.shape[0]):
        tend_ref[b] = tend[:, b * LANE : (b + 1) * LANE]


def backward_kernel(at_ref, x_ref, g_ref, a1_ref, a2_ref, *refs, cuts):
    *piece_refs, adj_ref, grad_ref, w_t_ref, w_ref, sum_ref = refs
    (in0, in1), (mid0, mid1), (out0, out1) = cuts

    @pl.when(pl.program_id(0) == 0)
    def _():
        place_weights(at_ref, piece_refs, w_t_ref, w_ref, [(0, out0)])
        sum_ref[...] = jnp.zeros_like(sum_ref)

    xf, scale, xn = normalised(wide(x_ref))
    g = wide(g_ref)
    a_two = a2_ref[...]
    sig = jax.nn.sigmoid(a_two)
    h_two = (a_two * sig).astype(BF16)
    d_two = (mul(w_t_ref[:, out0:out1], g) * (sig * (1.0 + a_two * (1.0 - sig)))).astype(BF16)
    sum_ref[:, out0:out1] += mul_slots(h_two, g)
    a_one = a1_ref[...]
    sig = jax.nn.sigmoid(a_one)
    h_one = (a_one * sig).astype(BF16)
    d_one = (mul(w_ref[mid0:mid1, :], d_two) * (sig * (1.0 + a_one * (1.0 - sig)))).astype(BF16)
    sum_ref[:, mid0:mid1] += mul_slots(d_two, h_one)
    d_norm = mul(w_ref[in0:in1, :], d_one)
    adj = (
        scale * d_norm - xf * (scale * scale * scale) * jnp.mean(xf * d_norm, axis=0, keepdims=True)
    ).astype(BF16)
    for b in range(x_ref.shape[0]):
        adj_ref[b] = adj[:, b * LANE : (b + 1) * LANE]
    sum_ref[:, in0:in1] += mul_slots(d_one, xn)

    @pl.when(pl.program_id(0) == pl.num_programs(0) - 1)
    def _():
        grad_ref[...] = sum_ref[...].astype(BF16)


def column_specs(shape, pieces):
    _, feat, length = shape
    rows, span = pieces[0].shape
    hid = rows * len(pieces)
    block = pl.BlockSpec((WIDE, feat, length), lambda i: (i, 0, 0))
    hidden = pl.BlockSpec((hid, WIDE * length), lambda i: (0, i))
    piece = pl.BlockSpec((rows, span), lambda i: (0, 0), pipeline_mode=pl.Buffered(1))
    return hid, span, block, hidden, [piece] * len(pieces)


def physics_forward(at, x, pieces, cuts):
    nblock, feat, length = x.shape
    hid, span, block, hidden, piece_specs = column_specs(x.shape, pieces)

    def kernel(*refs):
        forward_kernel(*refs, cuts=cuts)

    kept = jax.ShapeDtypeStruct((hid, nblock * length), F32)
    return pl.pallas_call(
        kernel,
        grid=(nblock // WIDE,),
        in_specs=[pl.BlockSpec(memory_space=pltpu.SMEM), block] + piece_specs,
        out_specs=[block, hidden, hidden],
        out_shape=[jax.ShapeDtypeStruct(x.shape, BF16), kept, kept],
        scratch_shapes=[pltpu.VMEM((hid, span), BF16), pltpu.VMEM((span - cuts[2][0], hid), BF16)],
        cost_estimate=pl.CostEstimate(
            flops=2 * hid * (2 * feat + hid) * nblock * length,
            transcendentals=4 * hid * nblock * length,
            bytes_accessed=x.size * 4 + hid * nblock * length * 8,
        ),
        name="physics_forward",
    )(at, x, *pieces)


def physics_backward(at, x, g, a_one, a_two, pieces, cuts):
    nblock, feat, length = x.shape
    hid, span, block, hidden, piece_specs = column_specs(x.shape, pieces)

    def kernel(*refs):
        backward_kernel(*refs, cuts=cuts)

    return pl.pallas_call(
        kernel,
        grid=(nblock // WIDE,),
        in_specs=[pl.BlockSpec(memory_space=pltpu.SMEM), block, block, hidden, hidden] + piece_specs,
        out_specs=[block, pl.BlockSpec((hid, span), lambda i: (0, 0))],
        out_shape=[jax.ShapeDtypeStruct(x.shape, BF16), jax.ShapeDtypeStruct((hid, span), BF16)],
        scratch_shapes=[
            pltpu.VMEM((hid, span), BF16),
            pltpu.VMEM((cuts[2][0], hid), BF16),
            pltpu.VMEM((hid, span), F32),
        ],
        cost_estimate=pl.CostEstimate(
            flops=4 * hid * (2 * feat + hid) * nblock * length,
            transcendentals=4 * hid * nblock * length,
            bytes_accessed=x.size * 6 + hid * nblock * length * 8,
        ),
        name="physics_backward",
    )(at, x, g, a_one, a_two, *pieces)


def plane(fields_ref, coef_refs, a, at):
    nfield = fields_ref.shape[0]
    return fields_ref[a, at, :] if a < nfield else coef_refs[a - nfield][at, :]


def inside(levels):
    return iota((GROUP, LANE), 0) + pl.program_id(0) * GROUP < levels


def rim_kernel(fields_ref, lon_ref, lat_ref, dif_ref, low_ref, high_ref, *, rows, levels):
    coefs = (lon_ref, lat_ref, dif_ref)
    keep = inside(levels)
    for r in range(STEPS):
        for a in range(low_ref.shape[1]):
            for first, out in ((r, low_ref), (rows - STEPS + r, high_ref)):
                value = plane(fields_ref, coefs, a, pl.ds(first, GROUP, stride=rows))
                out[r, a] = jnp.where(keep, value, 0.0).astype(BF16)


def strip_kernel(
    fields_ref, lon_ref, lat_ref, dif_ref, south_ref, north_ref, west_ref, east_ref, all_ref, sum_ref, *, rows, levels
):
    coefs = (lon_ref, lat_ref, dif_ref)
    planes = south_ref.shape[1]
    keep = inside(levels)
    for t in range(rows + 2 * STEPS):
        for a in range(planes):
            if t < STEPS:
                value = south_ref[t, a]
            elif t >= rows + STEPS:
                value = north_ref[t - rows - STEPS, a]
            else:
                own = plane(fields_ref, coefs, a, pl.ds(t - STEPS, GROUP, stride=rows))
                value = jnp.where(keep, own, 0.0).astype(BF16)
            all_ref[t * GROUP : (t + 1) * GROUP, a * LANE : (a + 1) * LANE] = value
    shape = (planes * LANE, 2 * LANE)
    k, n = iota(shape, 0), iota(shape, 1)
    a, q = k // LANE, k % LANE
    west = jnp.where(q < STEPS, STEPS * a + q, -1)
    east = jnp.where(q >= LANE - STEPS, STEPS * a + q - (LANE - STEPS) + LANE, -1)
    pick = jnp.where((n == west) | (n == east), 1.0, 0.0).astype(BF16)
    got = jnp.dot(all_ref[...], pick, preferred_element_type=F32)
    group = pl.program_id(0)

    @pl.when(group == 0)
    def _():
        sum_ref[...] = got

    @pl.when(group > 0)
    def _():
        for half in range(2):
            part = got[:, half * LANE : (half + 1) * LANE]
            sum_ref[:, half * LANE : (half + 1) * LANE] += pltpu.roll(part, group * GROUP, 1)

    @pl.when(group == pl.num_programs(0) - 1)
    def _():
        west_ref[...] = sum_ref[:, :LANE].astype(BF16)
        east_ref[...] = sum_ref[:, LANE:].astype(BF16)


def weights_of(c_lon, c_lat, c_dif):
    return (
        1.0 - 4.0 * c_dif,
        c_dif - 0.5 * c_lon,
        c_dif + 0.5 * c_lon,
        c_dif - 0.5 * c_lat,
        c_dif + 0.5 * c_lat,
    )


def stepped(coef, centre, east, west, north, south):
    return coef[0] * centre + (coef[1] * east + coef[2] * west) + (coef[3] * north + coef[4] * south)


def dynamics_kernel(
    fields_ref,
    lon_ref,
    lat_ref,
    dif_ref,
    south_ref,
    north_ref,
    own_w_ref,
    own_e_ref,
    from_e_ref,
    from_w_ref,
    out_ref,
    rim_ref,
    strip_ref,
    coef_ref,
    join_ref,
    state_ref,
    shift_ref,
    *,
    rows,
    first,
):
    coefs = (lon_ref, lat_ref, dif_ref)
    nfield = fields_ref.shape[0]
    total = rows + 2 * STEPS
    rim_ref[0] = south_ref[...].astype(F32)
    rim_ref[1] = north_ref[...].astype(F32)

    sources = jnp.concatenate([own_e_ref[...], from_e_ref[...], from_w_ref[...], own_w_ref[...]], axis=1)
    shape = (4 * LANE, 4 * LANE)
    k, n = iota(shape, 0), iota(shape, 1)
    lane, kind, m = k % LANE, n // LANE, n % LANE
    row_code = (k // LANE) * STEPS + lane % STEPS + 16 * ((lane // STEPS) % 8)
    row_code = jnp.where(lane // GROUP == pl.program_id(0) + first, row_code, -1)
    col_code = jnp.where(kind == 0, m, m % 16 + 16 * (nfield - 1 + kind))
    col_code = jnp.where(m < 16 * nfield, col_code, -2)
    pick = jnp.where(row_code == col_code, 1.0, 0.0).astype(BF16)
    strip_ref[...] = jnp.dot(sources, pick, preferred_element_type=F32)

    @pl.when(pl.program_id(0) == 0)
    def _():
        shape = (2 * LANE, 2 * LANE)
        k, n = iota(shape, 0), iota(shape, 1)
        east = jnp.where(k < LANE, k - 1, jnp.where(k % 16 == 4, LANE - 1, -1))
        west = jnp.where(k < LANE - 1, k + 1 + LANE, jnp.where((k >= LANE) & (k % 16 == 11), LANE, -1))
        shift_ref[...] = jnp.where(((n == east) & (k > 0)) | (n == west), 1.0, 0.0).astype(BF16)

    part = LEVELS
    lane = iota((part, LANE), 1)
    of_field = [jnp.where(lane // 16 == f, 1.0, 0.0).astype(BF16) for f in range(nfield)]

    def levels(sub, carry):
        def cell(a, t):
            if STEPS <= t < rows + STEPS:
                return plane(fields_ref, coefs, a, pl.ds(sub * (part * rows) + t - STEPS, part, stride=rows))
            side, at = (0, t) if t < STEPS else (1, t - rows - STEPS)
            return rim_ref[side, at, a, pl.ds(sub * part, part), :]

        def strip(kind, t):
            return strip_ref[pl.ds(t * GROUP + sub * part, part), kind * LANE : (kind + 1) * LANE]

        for t in range(1, total - 1):
            at = slice(t * part, (t + 1) * part)
            for c, value in enumerate(weights_of(cell(nfield, t), cell(nfield + 1, t), cell(nfield + 2, t))):
                coef_ref[0, c, at] = value
            for c, value in enumerate(weights_of(strip(1, t), strip(2, t), strip(3, t))):
                coef_ref[1, c, at] = value
        for f in range(nfield):
            for t in range(total):
                state_ref[0, f, t * part : (t + 1) * part] = cell(f, t)

        state = {t: strip(0, t) for t in range(total)}
        for step in range(STEPS):
            inner = range(step + 1, total - 1 - step)
            for t in inner:
                narrow = state[t].astype(BF16)
                for f in range(nfield):
                    join_ref[step, f, t * part : (t + 1) * part] = narrow * of_field[f]
            if step < STEPS - 1:
                state = {
                    t: stepped(
                        [coef_ref[1, c, t * part : (t + 1) * part] for c in range(5)],
                        state[t],
                        pltpu.roll(state[t], LANE - 1, 1),
                        pltpu.roll(state[t], 1, 1),
                        state[t + 1],
                        state[t - 1],
                    )
                    for t in inner
                }

        def rows_of(step, by=0):
            return slice((step + 1 + by) * part, (total - 1 - step + by) * part)

        def neighbours(step, pair):
            at = rows_of(step)
            cells = [
                jnp.concatenate([state_ref[step % 2, f, at].astype(BF16), join_ref[step, f, at]], axis=1) for f in pair
            ]
            return mul(jnp.concatenate(cells, axis=0), shift_ref[...])

        turns = [(step, pair) for step in range(STEPS) for pair in ((0, 1), (2, 3))]
        ready = neighbours(*turns[0])
        for turn, (step, pair) in enumerate(turns):
            sides = ready
            if turn + 1 < len(turns):
                ready = neighbours(*turns[turn + 1])
            size = (total - 2 - 2 * step) * part
            cur = step % 2
            for u in range(step + 1, total - 1 - step):
                at, side = slice(u * part, (u + 1) * part), (u - step - 1) * part
                coef = [coef_ref[0, c, at] for c in range(5)]
                for n, f in enumerate(pair):
                    value = stepped(
                        coef,
                        state_ref[cur, f, at],
                        sides[n * size + side : n * size + side + part, :LANE],
                        sides[n * size + side : n * size + side + part, LANE:],
                        state_ref[cur, f, (u + 1) * part : (u + 2) * part],
                        state_ref[cur, f, (u - 1) * part : u * part],
                    )
                    if step < STEPS - 1:
                        state_ref[1 - cur, f, at] = value
                    else:
                        out_ref[f, pl.ds(sub * (part * rows) + u - STEPS, part, stride=rows), :] = value
        return carry

    lax.fori_loop(0, GROUP // part, levels, 0)


class Dynamics:
    def __init__(self, fields, coefs, rows, levels):
        self.args = (fields, *coefs)
        self.rows, self.levels = rows, levels
        nfield = fields.shape[0]
        planes = nfield + len(coefs)
        groups = pl.cdiv(levels, GROUP)
        self.grid = (groups,)
        self.planes = planes
        self.strip_rows = (rows + 2 * STEPS) * GROUP
        self.fields_spec = pl.BlockSpec((nfield, GROUP * rows, LANE), lambda i: (0, i, 0))
        self.arg_specs = [self.fields_spec] + [pl.BlockSpec((GROUP * rows, LANE), lambda i: (i, 0))] * 3
        self.rim_spec = pl.BlockSpec((STEPS, planes, GROUP, LANE), lambda i: (0, 0, i, 0))
        self.rim_shape = jax.ShapeDtypeStruct((STEPS, planes, groups * GROUP, LANE), BF16)
        self.strip_spec = pl.BlockSpec((self.strip_rows, LANE), lambda i: (0, 0))
        self.strip_shape = jax.ShapeDtypeStruct((self.strip_rows, LANE), BF16)

    def rims(self, start):
        def kernel(*refs):
            rim_kernel(*refs, rows=self.rows, levels=self.levels)

        return pl.pallas_call(
            kernel,
            grid=self.grid,
            in_specs=self.arg_specs,
            out_specs=[self.rim_spec, self.rim_spec],
            out_shape=[self.rim_shape, self.rim_shape],
            name="rims",
        )(self.args[0], *after(self.args[1:], start))

    def send_rims(self, low, high):
        size = lax.axis_size("lat")
        up = [(i, i + 1) for i in range(size - 1)]
        south = lax.ppermute(high, "lat", up)
        north = lax.ppermute(low, "lat", [(j, i) for i, j in up])
        return south, north

    def strips(self, south, north, start):
        def kernel(*refs):
            strip_kernel(*refs, rows=self.rows, levels=self.levels)

        south, north = after((south, north), start)
        return pl.pallas_call(
            kernel,
            grid=self.grid,
            in_specs=self.arg_specs + [self.rim_spec, self.rim_spec],
            out_specs=[self.strip_spec, self.strip_spec],
            out_shape=[self.strip_shape, self.strip_shape],
            scratch_shapes=[
                pltpu.VMEM((self.strip_rows, self.planes * LANE), BF16),
                pltpu.VMEM((self.strip_rows, 2 * LANE), F32),
            ],
            name="strips",
        )(*self.args, south, north)

    def send_strips(self, own_w, own_e):
        size = lax.axis_size("lon")
        around = [(i, (i + 1) % size) for i in range(size)]
        from_w = lax.ppermute(own_e, "lon", around)
        from_e = lax.ppermute(own_w, "lon", [(j, i) for i, j in around])
        return from_w, from_e

    def steps(self, first, count, rims, strips, start, state=None):
        def kernel(*refs):
            inputs = refs[:10]
            dynamics_kernel(*inputs, *refs[10 + (state is not None) :], rows=self.rows, first=first)

        fields = self.args[0]
        nfield = fields.shape[0]
        chunk = GROUP * self.rows
        fields_spec = pl.BlockSpec((nfield, chunk, LANE), lambda i: (0, i + first, 0))
        coef_spec = pl.BlockSpec((chunk, LANE), lambda i: (i + first, 0))
        rim_spec = pl.BlockSpec((STEPS, self.planes, GROUP, LANE), lambda i: (0, 0, i + first, 0))
        specs = [fields_spec] + [coef_spec] * 3 + [rim_spec] * 2 + [self.strip_spec] * 4
        operands = self.args + rims + after(strips, start)
        aliases = {}
        if state is not None:
            specs.append(pl.BlockSpec(memory_space=pl.ANY))
            aliases = {len(operands): 0}
            operands += (state,)
        cells = (self.rows + 2 * STEPS) * LEVELS
        return pl.pallas_call(
            kernel,
            grid=(count,),
            in_specs=specs,
            out_specs=fields_spec,
            out_shape=jax.ShapeDtypeStruct(fields.shape, F32),
            input_output_aliases=aliases,
            scratch_shapes=[
                pltpu.VMEM((2, STEPS, self.planes, GROUP, LANE), F32),
                pltpu.VMEM((self.strip_rows, 4 * LANE), F32),
                pltpu.VMEM((2, 5, cells, LANE), F32),
                pltpu.VMEM((STEPS, nfield, cells, LANE), BF16),
                pltpu.VMEM((2, nfield, cells, LANE), F32),
                pltpu.VMEM((2 * LANE, 2 * LANE), BF16),
            ],
            cost_estimate=pl.CostEstimate(
                flops=fields.size * 60 * count // self.grid[0],
                transcendentals=0,
                bytes_accessed=fields.size * 11 * count // self.grid[0],
            ),
            name="dynamics",
        )(*operands)


def after(values, start):
    return lax.optimization_barrier((values, start))[0]


def exchange(array, axis):
    return lax.all_to_all(array, axis, split_axis=0, concat_axis=0, tiled=True)


def spread(piece):
    size = lax.axis_size("lat")
    other = lax.ppermute(piece, "lat", [(i, i ^ 1) for i in range(size)])
    both = jnp.concatenate([piece, other], axis=0)
    pieces = [both]
    for shift in range(1, size // 2):
        pieces.append(lax.ppermute(both, "lat", [(i, (i + 2 * shift) % size) for i in range(size)]))
    return pieces


def scattered(parts, start):
    size = parts.shape[0]
    core = lax.axis_index("lat") % 2
    pairs = parts.reshape((size // 2, 2) + parts.shape[1:])
    mine = lax.dynamic_index_in_dim(pairs, core, 1, keepdims=False)
    other = lax.dynamic_index_in_dim(pairs, 1 - core, 1, keepdims=False)
    other = lax.ppermute(other, "lat", [(i, i ^ 1) for i in range(size)])
    both = mine.astype(F32) + other.astype(F32)
    chips = size // 2
    chip = lax.axis_index("lat") // 2
    total = lax.dynamic_index_in_dim(both, chip, 0, keepdims=False)
    both = after(both.astype(BF16), start)
    for shift in range(1, chips):
        part = lax.dynamic_index_in_dim(both, (chip + shift) % chips, 0, keepdims=False)
        to = [(i, (i + 2 * shift) % size) for i in range(size)]
        total = total + lax.ppermute(part, "lat", to).astype(F32)
    return total


def shards(
    fields,
    courant_lon,
    courant_lat,
    diffusion,
    tend_cot,
    col_list,
    block_count,
    block_dest,
    w_in,
    w_mid,
    w_out,
):
    nfield, levels, rows, columns = fields.shape
    feat = nfield * levels
    hid_mid, hid_own = w_mid.shape[1:]
    nlat = lax.axis_size("lat")
    pad = -feat % LANE
    cuts = (
        (0, feat),
        (feat + pad, feat + pad + hid_mid),
        (feat + pad + hid_mid, 2 * feat + pad + hid_mid),
    )
    span = cuts[2][1] + pad

    coefs = [c.reshape(levels * rows, columns) for c in (courant_lon, courant_lat, diffusion)]
    window = Dynamics(fields.reshape(nfield, levels * rows, columns), coefs, rows, levels)

    nblock = block_dest.shape[-1]
    cols = col_list.reshape(nblock, 1, LANE)
    send_x, table = gather_first(block_dest, block_count, cols, fields.reshape(feat * rows, columns), feat, rows)
    recv_x = exchange(send_x, "lon")
    rest = jnp.zeros((pad, hid_own), BF16)
    own = jnp.concatenate([w_in[0], rest, w_mid[0], w_out[0], rest], axis=0).T
    pieces = spread(after(own, send_x))
    lat = lax.axis_index("lat")
    at = jnp.stack([lat // 2, lat % 2]).astype(jnp.int32)
    low, high = window.rims(send_x)
    south, north = window.send_rims(low, high)
    send_g = gather_columns(after(table, low), tend_cot.reshape(feat * rows, columns), feat, rows)
    recv_g = exchange(send_g, "lon")
    own_w, own_e = window.strips(south, north, send_g)
    from_w, from_e = window.send_strips(own_w, own_e)
    tend, a_one, a_two = physics_forward(at, after(recv_x, own_w), pieces, cuts)
    back_tend = exchange(tend, "lon")
    adj, grads = physics_backward(at, recv_x, recv_g, a_one, a_two, pieces, cuts)
    rims, strips = (south, north), (own_w, own_e, from_e, from_w)
    last = window.grid[0] - 1
    state = window.steps(last, 1, rims, strips, adj)
    back_adj = exchange(after(adj, back_tend), "lon")
    state = window.steps(0, last, rims, strips, back_tend, state)
    summed = scattered(grads.reshape(nlat, hid_own, span), back_tend).T
    grad_in, grad_mid, grad_out = (summed[a:b][None] for a, b in cuts)

    new_fields = scatter_columns(table, back_tend, rows, state.reshape(feat * rows, columns))
    adjoint = scatter_columns(table, back_adj, rows)
    return (new_fields.reshape(fields.shape), adjoint.reshape(fields.shape), grad_in, grad_mid, grad_out)


def solution(mesh):
    return jax.shard_map(
        shards,
        mesh=mesh,
        in_specs=(
            P(None, None, "lat", "lon"),
            P(None, "lat", "lon"),
            P(None, "lat", "lon"),
            P(None, "lat", "lon"),
            P(None, None, "lat", "lon"),
            P("lat", "lon", None),
            P("lat", "lon", None),
            P("lat", "lon", None),
            P("lon", None, "lat"),
            P("lon", None, "lat"),
            P("lon", None, "lat"),
        ),
        out_specs=(
            P(None, None, "lat", "lon"),
            P(None, None, "lat", "lon"),
            P("lon", None, "lat"),
            P("lon", None, "lat"),
            P("lon", None, "lat"),
        ),
        check_vma=False,
    )
```

```python
import jax
import jax.numpy as jnp
from jax import lax
from jax.experimental import pallas as pl
from jax.experimental.pallas import tpu as pltpu
from jax.sharding import PartitionSpec as P


STEPS = 4
LANE = 128
WIDE = 4
GROUP = 32
LEVELS = 16
F32 = jnp.float32
BF16 = jnp.bfloat16


def iota(shape, dim):
    return lax.broadcasted_iota(jnp.int32, shape, dim)


def rows_of_source(src_ref, mat_ref, rows):
    for r in range(rows):
        mat_ref[:, r * LANE : (r + 1) * LANE] = src_ref[pl.ds(r, mat_ref.shape[0], stride=rows), :].astype(BF16)


def gather_blocks(table_ref, mat_ref, out_ref):
    ncol = mat_ref.shape[1]
    first = pl.program_id(0) * WIDE
    column = iota((ncol, LANE), 0)
    hot = [jnp.where(column == table_ref[pl.ds(first + b, 1), :], 1.0, 0.0).astype(BF16) for b in range(WIDE)]
    got = jnp.dot(mat_ref[...], jnp.concatenate(hot, axis=1), preferred_element_type=F32).astype(BF16)
    for b in range(WIDE):
        out_ref[b] = got[:, b * LANE : (b + 1) * LANE]


def gather_first_kernel(dest_ref, count_ref, cols_ref, src_ref, out_ref, table_ref, mat_ref, full_ref, sems, *, rows):
    feat = mat_ref.shape[0]

    @pl.when(pl.program_id(0) == 0)
    def _():
        cuts = [(start, min(start + LANE, feat)) for start in range(0, feat, LANE)]
        loads = []
        for n, (start, stop) in enumerate(cuts):
            at = pl.ds(start * rows, (stop - start) * rows)
            loads.append(pltpu.make_async_copy(src_ref.at[at], full_ref.at[at], sems.at[n]))
            loads[-1].start()
        slot = iota((1, LANE), 1)
        for b in range(cols_ref.shape[0]):
            row = jnp.where(slot < count_ref[0, 0, b], cols_ref[b], -1)
            table_ref[pl.ds(dest_ref[0, 0, b], 1), :] = row
        for load, (start, stop) in zip(loads, cuts):
            load.wait()
            for r in range(rows):
                part = full_ref[pl.ds(start * rows + r, stop - start, stride=rows), :]
                mat_ref[start:stop, r * LANE : (r + 1) * LANE] = part.astype(BF16)

    gather_blocks(table_ref, mat_ref, out_ref)


def gather_kernel(table_ref, src_ref, out_ref, mat_ref, wide_ref, *, rows):
    @pl.when(pl.program_id(0) == 0)
    def _():
        wide_ref[...] = src_ref[...].astype(F32)
        rows_of_source(wide_ref, mat_ref, rows)

    gather_blocks(table_ref, mat_ref, out_ref)


def gather_parts(source, nblock, feat, rows):
    once = pl.BlockSpec(source.shape, lambda i: (0, 0), pipeline_mode=pl.Buffered(1))
    out = pl.BlockSpec((WIDE, feat, LANE), lambda i: (i, 0, 0))
    shape = jax.ShapeDtypeStruct((nblock, feat, LANE), BF16)
    cost = pl.CostEstimate(
        flops=2 * feat * rows * LANE * nblock * LANE,
        transcendentals=0,
        bytes_accessed=source.size * source.dtype.itemsize + feat * nblock * LANE * 2,
    )
    return once, out, shape, cost


def gather_first(dest, count, cols, source, feat, rows):
    nblock = cols.shape[0]
    _, out, shape, cost = gather_parts(source, nblock, feat, rows)
    table = jax.ShapeDtypeStruct((nblock, LANE), jnp.int32)

    def kernel(*refs):
        gather_first_kernel(*refs, rows=rows)

    scalars = pl.BlockSpec(memory_space=pltpu.SMEM)
    return pl.pallas_call(
        kernel,
        grid=(nblock // WIDE,),
        in_specs=[scalars, scalars, pl.BlockSpec(cols.shape, lambda i: (0, 0, 0)), pl.BlockSpec(memory_space=pl.ANY)],
        out_specs=[out, pl.BlockSpec(table.shape, lambda i: (0, 0))],
        out_shape=[shape, table],
        scratch_shapes=[
            pltpu.VMEM((feat, rows * LANE), BF16),
            pltpu.VMEM(source.shape, F32),
            pltpu.SemaphoreType.DMA((pl.cdiv(feat, LANE),)),
        ],
        cost_estimate=cost,
        name="gather_first",
    )(dest, count, cols, source)


def gather_columns(table, source, feat, rows):
    nblock = table.shape[0]
    once, out, shape, cost = gather_parts(source, nblock, feat, rows)

    def kernel(*refs):
        gather_kernel(*refs, rows=rows)

    return pl.pallas_call(
        kernel,
        grid=(nblock // WIDE,),
        in_specs=[pl.BlockSpec(table.shape, lambda i: (0, 0)), once],
        out_specs=out,
        out_shape=shape,
        scratch_shapes=[pltpu.VMEM((feat, rows * LANE), BF16), pltpu.VMEM(source.shape, F32)],
        cost_estimate=cost,
        name="gather_columns",
    )(table, source)


def scatter_rows(table_ref, blocks_ref, mat_ref, where_ref):
    nblock = blocks_ref.shape[0]

    @pl.when(pl.program_id(0) == 0)
    def _():
        table = table_ref[...].astype(F32)
        by_slot = jnp.concatenate([table, jnp.zeros((LANE - nblock, LANE), F32)], axis=0).T
        for b in range(nblock):
            mat_ref[:, b * LANE : (b + 1) * LANE] = blocks_ref[b]
            column = jnp.broadcast_to(by_slot[:, b : b + 1], (LANE, LANE))
            where_ref[b * LANE : (b + 1) * LANE, :] = column.astype(jnp.int32)

    where = where_ref[...]
    lane = iota(where.shape, 1) + pl.program_id(0) * (WIDE * LANE)
    hot = [jnp.where(where == lane + r * LANE, 1.0, 0.0).astype(BF16) for r in range(WIDE)]
    return jnp.dot(mat_ref[...], jnp.concatenate(hot, axis=1), preferred_element_type=F32)


def scatter_add_kernel(table_ref, blocks_ref, base_ref, out_ref, mat_ref, where_ref, *, rows):
    got = scatter_rows(table_ref, blocks_ref, mat_ref, where_ref)
    for r in range(WIDE):
        at = pl.ds(pl.program_id(0) * WIDE + r, mat_ref.shape[0], stride=rows)
        out_ref[at, :] = base_ref[at, :] + got[:, r * LANE : (r + 1) * LANE]


def scatter_kernel(table_ref, blocks_ref, out_ref, mat_ref, where_ref, full_ref, *, rows):
    got = scatter_rows(table_ref, blocks_ref, mat_ref, where_ref)
    for r in range(WIDE):
        at = pl.ds(pl.program_id(0) * WIDE + r, mat_ref.shape[0], stride=rows)
        full_ref[at, :] = got[:, r * LANE : (r + 1) * LANE]

    @pl.when(pl.program_id(0) == pl.num_programs(0) - 1)
    def _():
        out_ref[...] = full_ref[...].astype(BF16)


def scatter_columns(table, blocks, rows, base=None):
    nblock, feat, length = blocks.shape
    nslot = nblock * length
    shape = (feat * rows, LANE)
    whole = pl.BlockSpec(shape, lambda i: (0, 0), pipeline_mode=pl.Buffered(1))
    specs = [
        pl.BlockSpec(table.shape, lambda i: (0, 0)),
        pl.BlockSpec(blocks.shape, lambda i: (0, 0, 0), pipeline_mode=pl.Buffered(1)),
    ]
    scratch = [pltpu.VMEM((feat, nslot), BF16), pltpu.VMEM((nslot, LANE), jnp.int32)]
    if base is None:
        body, operands, dtype = scatter_kernel, (table, blocks), BF16
        scratch.append(pltpu.VMEM(shape, F32))
    else:
        body, operands, dtype = scatter_add_kernel, (table, blocks, base), F32
        specs.append(whole)

    def kernel(*refs):
        body(*refs, rows=rows)

    return pl.pallas_call(
        kernel,
        grid=(rows // WIDE,),
        in_specs=specs,
        out_specs=pl.BlockSpec(shape, lambda i: (0, 0)),
        out_shape=jax.ShapeDtypeStruct(shape, dtype),
        scratch_shapes=scratch,
        cost_estimate=pl.CostEstimate(
            flops=2 * feat * nslot * rows * LANE, transcendentals=0, bytes_accessed=feat * nslot * 8
        ),
        name="scatter_columns",
    )(*operands)


def wide(ref):
    return jnp.concatenate([ref[b] for b in range(ref.shape[0])], axis=1)


def normalised(x):
    xf = x.astype(F32)
    scale = lax.rsqrt(jnp.mean(xf * xf, axis=0, keepdims=True) + 1e-06)
    return xf, scale, (xf * scale).astype(BF16)


def mul(a, b):
    return jnp.dot(a, b, preferred_element_type=F32)


def mul_slots(a, b):
    return lax.dot_general(a, b, (((1,), (1,)), ((), ())), preferred_element_type=F32)


def place_weights(at_ref, piece_refs, w_t_ref, w_ref, parts):
    size = piece_refs[0].shape[0] // 2
    pieces = [ref.at[k : k + size] for ref in piece_refs for k in range(0, ref.shape[0], size)]
    for n, piece in enumerate(pieces):
        place = 2 * (at_ref[0] ^ (n // 2)) + (at_ref[1] ^ (n % 2))
        w_t_ref[pl.ds(pl.multiple_of(place * size, size), size), :] = piece[...]
    row = 0
    for start, stop in parts:
        w_ref[row : row + stop - start, :] = w_t_ref[:, start:stop].T
        row += stop - start


def forward_kernel(at_ref, x_ref, *refs, cuts):
    *piece_refs, tend_ref, a1_ref, a2_ref, w_t_ref, w_ref = refs
    (in0, in1), (mid0, mid1), (out0, out1) = cuts

    @pl.when(pl.program_id(0) == 0)
    def _():
        place_weights(at_ref, piece_refs, w_t_ref, w_ref, [(out0, w_t_ref.shape[1])])

    _, _, xn = normalised(wide(x_ref))
    a_one = mul(w_t_ref[:, in0:in1], xn)
    a1_ref[...] = a_one
    h_one = (a_one * jax.nn.sigmoid(a_one)).astype(BF16)
    a_two = mul(w_t_ref[:, mid0:mid1], h_one)
    a2_ref[...] = a_two
    h_two = (a_two * jax.nn.sigmoid(a_two)).astype(BF16)
    tend = mul(w_ref[: out1 - out0, :], h_two).astype(BF16)
    for b in range(x_ref.shape[0]):
        tend_ref[b] = tend[:, b * LANE : (b + 1) * LANE]


def backward_kernel(at_ref, x_ref, g_ref, a1_ref, a2_ref, *refs, cuts):
    *piece_refs, adj_ref, grad_ref, w_t_ref, w_ref, sum_ref = refs
    (in0, in1), (mid0, mid1), (out0, out1) = cuts

    @pl.when(pl.program_id(0) == 0)
    def _():
        place_weights(at_ref, piece_refs, w_t_ref, w_ref, [(0, out0)])
        sum_ref[...] = jnp.zeros_like(sum_ref)

    xf, scale, xn = normalised(wide(x_ref))
    g = wide(g_ref)
    a_two = a2_ref[...]
    sig = jax.nn.sigmoid(a_two)
    h_two = (a_two * sig).astype(BF16)
    d_two = (mul(w_t_ref[:, out0:out1], g) * (sig * (1.0 + a_two * (1.0 - sig)))).astype(BF16)
    sum_ref[:, out0:out1] += mul_slots(h_two, g)
    a_one = a1_ref[...]
    sig = jax.nn.sigmoid(a_one)
    h_one = (a_one * sig).astype(BF16)
    d_one = (mul(w_ref[mid0:mid1, :], d_two) * (sig * (1.0 + a_one * (1.0 - sig)))).astype(BF16)
    sum_ref[:, mid0:mid1] += mul_slots(d_two, h_one)
    d_norm = mul(w_ref[in0:in1, :], d_one)
    adj = (
        scale * d_norm - xf * (scale * scale * scale) * jnp.mean(xf * d_norm, axis=0, keepdims=True)
    ).astype(BF16)
    for b in range(x_ref.shape[0]):
        adj_ref[b] = adj[:, b * LANE : (b + 1) * LANE]
    sum_ref[:, in0:in1] += mul_slots(d_one, xn)

    @pl.when(pl.program_id(0) == pl.num_programs(0) - 1)
    def _():
        grad_ref[...] = sum_ref[...].astype(BF16)


def column_specs(shape, pieces):
    _, feat, length = shape
    span = pieces[0].shape[1]
    hid = sum(piece.shape[0] for piece in pieces)
    block = pl.BlockSpec((WIDE, feat, length), lambda i: (i, 0, 0))
    hidden = pl.BlockSpec((hid, WIDE * length), lambda i: (0, i))
    specs = [pl.BlockSpec(piece.shape, lambda i: (0, 0), pipeline_mode=pl.Buffered(1)) for piece in pieces]
    return hid, span, block, hidden, specs


def physics_forward(at, x, pieces, cuts):
    nblock, feat, length = x.shape
    hid, span, block, hidden, piece_specs = column_specs(x.shape, pieces)

    def kernel(*refs):
        forward_kernel(*refs, cuts=cuts)

    kept = jax.ShapeDtypeStruct((hid, nblock * length), F32)
    return pl.pallas_call(
        kernel,
        grid=(nblock // WIDE,),
        in_specs=[pl.BlockSpec(memory_space=pltpu.SMEM), block] + piece_specs,
        out_specs=[block, hidden, hidden],
        out_shape=[jax.ShapeDtypeStruct(x.shape, BF16), kept, kept],
        scratch_shapes=[pltpu.VMEM((hid, span), BF16), pltpu.VMEM((span - cuts[2][0], hid), BF16)],
        cost_estimate=pl.CostEstimate(
            flops=2 * hid * (2 * feat + hid) * nblock * length,
            transcendentals=4 * hid * nblock * length,
            bytes_accessed=x.size * 4 + hid * nblock * length * 8,
        ),
        name="physics_forward",
    )(at, x, *pieces)


def physics_backward(at, x, g, a_one, a_two, pieces, cuts):
    nblock, feat, length = x.shape
    hid, span, block, hidden, piece_specs = column_specs(x.shape, pieces)

    def kernel(*refs):
        backward_kernel(*refs, cuts=cuts)

    return pl.pallas_call(
        kernel,
        grid=(nblock // WIDE,),
        in_specs=[pl.BlockSpec(memory_space=pltpu.SMEM), block, block, hidden, hidden] + piece_specs,
        out_specs=[block, pl.BlockSpec((hid, span), lambda i: (0, 0))],
        out_shape=[jax.ShapeDtypeStruct(x.shape, BF16), jax.ShapeDtypeStruct((hid, span), BF16)],
        scratch_shapes=[
            pltpu.VMEM((hid, span), BF16),
            pltpu.VMEM((cuts[2][0], hid), BF16),
            pltpu.VMEM((hid, span), F32),
        ],
        cost_estimate=pl.CostEstimate(
            flops=4 * hid * (2 * feat + hid) * nblock * length,
            transcendentals=4 * hid * nblock * length,
            bytes_accessed=x.size * 6 + hid * nblock * length * 8,
        ),
        name="physics_backward",
    )(at, x, g, a_one, a_two, *pieces)


def plane(fields_ref, coef_refs, a, at):
    nfield = fields_ref.shape[0]
    return fields_ref[a, at, :] if a < nfield else coef_refs[a - nfield][at, :]


def inside(levels):
    return iota((GROUP, LANE), 0) + pl.program_id(0) * GROUP < levels


def rim_kernel(fields_ref, lon_ref, lat_ref, dif_ref, low_ref, high_ref, *, rows, levels):
    coefs = (lon_ref, lat_ref, dif_ref)
    keep = inside(levels)
    for r in range(STEPS):
        for a in range(low_ref.shape[1]):
            for first, out in ((r, low_ref), (rows - STEPS + r, high_ref)):
                value = plane(fields_ref, coefs, a, pl.ds(first, GROUP, stride=rows))
                out[r, a] = jnp.where(keep, value, 0.0).astype(BF16)


def strip_kernel(
    fields_ref, lon_ref, lat_ref, dif_ref, south_ref, north_ref, west_ref, east_ref, all_ref, sum_ref, *, rows, levels
):
    coefs = (lon_ref, lat_ref, dif_ref)
    planes = south_ref.shape[1]
    keep = inside(levels)
    for t in range(rows + 2 * STEPS):
        for a in range(planes):
            if t < STEPS:
                value = south_ref[t, a]
            elif t >= rows + STEPS:
                value = north_ref[t - rows - STEPS, a]
            else:
                own = plane(fields_ref, coefs, a, pl.ds(t - STEPS, GROUP, stride=rows))
                value = jnp.where(keep, own, 0.0).astype(BF16)
            all_ref[t * GROUP : (t + 1) * GROUP, a * LANE : (a + 1) * LANE] = value
    shape = (planes * LANE, 2 * LANE)
    k, n = iota(shape, 0), iota(shape, 1)
    a, q = k // LANE, k % LANE
    west = jnp.where(q < STEPS, STEPS * a + q, -1)
    east = jnp.where(q >= LANE - STEPS, STEPS * a + q - (LANE - STEPS) + LANE, -1)
    pick = jnp.where((n == west) | (n == east), 1.0, 0.0).astype(BF16)
    got = jnp.dot(all_ref[...], pick, preferred_element_type=F32)
    group = pl.program_id(0)

    @pl.when(group == 0)
    def _():
        sum_ref[...] = got

    @pl.when(group > 0)
    def _():
        for half in range(2):
            part = got[:, half * LANE : (half + 1) * LANE]
            sum_ref[:, half * LANE : (half + 1) * LANE] += pltpu.roll(part, group * GROUP, 1)

    @pl.when(group == pl.num_programs(0) - 1)
    def _():
        west_ref[...] = sum_ref[:, :LANE].astype(BF16)
        east_ref[...] = sum_ref[:, LANE:].astype(BF16)


def weights_of(c_lon, c_lat, c_dif):
    return (
        1.0 - 4.0 * c_dif,
        c_dif - 0.5 * c_lon,
        c_dif + 0.5 * c_lon,
        c_dif - 0.5 * c_lat,
        c_dif + 0.5 * c_lat,
    )


def stepped(coef, centre, east, west, north, south):
    return coef[0] * centre + (coef[1] * east + coef[2] * west) + (coef[3] * north + coef[4] * south)


def dynamics_kernel(
    fields_ref,
    lon_ref,
    lat_ref,
    dif_ref,
    south_ref,
    north_ref,
    own_w_ref,
    own_e_ref,
    from_e_ref,
    from_w_ref,
    out_ref,
    rim_ref,
    strip_ref,
    coef_ref,
    join_ref,
    state_ref,
    shift_ref,
    *,
    rows,
    first,
):
    coefs = (lon_ref, lat_ref, dif_ref)
    nfield = fields_ref.shape[0]
    total = rows + 2 * STEPS
    rim_ref[0] = south_ref[...].astype(F32)
    rim_ref[1] = north_ref[...].astype(F32)

    sources = jnp.concatenate([own_e_ref[...], from_e_ref[...], from_w_ref[...], own_w_ref[...]], axis=1)
    k = iota((4 * LANE, LANE), 0)
    lane = k % LANE
    row_code = (k // LANE) * STEPS + lane % STEPS + 16 * ((lane // STEPS) % 8)
    row_code = jnp.where(lane // GROUP == pl.program_id(0) + first, row_code, -1)
    m = iota((1, LANE), 1)
    picks = []
    for kind in range(4):
        col_code = m if kind == 0 else m % 16 + 16 * (nfield - 1 + kind)
        col_code = jnp.where(m < 16 * nfield, col_code, -2)
        picks.append(jnp.where(row_code == col_code, 1.0, 0.0).astype(BF16))
    pick = jnp.concatenate(picks, axis=1)
    strip_ref[...] = jnp.dot(sources, pick, preferred_element_type=F32)

    @pl.when(pl.program_id(0) == 0)
    def _():
        shape = (2 * LANE, 2 * LANE)
        k, n = iota(shape, 0), iota(shape, 1)
        east = jnp.where(k < LANE, k - 1, jnp.where(k % 16 == 4, LANE - 1, -1))
        west = jnp.where(k < LANE - 1, k + 1 + LANE, jnp.where((k >= LANE) & (k % 16 == 11), LANE, -1))
        shift_ref[...] = jnp.where(((n == east) & (k > 0)) | (n == west), 1.0, 0.0).astype(BF16)

    part = LEVELS
    lane = iota((part, LANE), 1)
    of_field = [jnp.where(lane // 16 == f, 1.0, 0.0).astype(BF16) for f in range(nfield)]

    def levels(sub, carry):
        def cell(a, t):
            if STEPS <= t < rows + STEPS:
                return plane(fields_ref, coefs, a, pl.ds(sub * (part * rows) + t - STEPS, part, stride=rows))
            side, at = (0, t) if t < STEPS else (1, t - rows - STEPS)
            return rim_ref[side, at, a, pl.ds(sub * part, part), :]

        def strip(kind, t):
            return strip_ref[pl.ds(t * GROUP + sub * part, part), kind * LANE : (kind + 1) * LANE]

        for t in range(1, total - 1):
            at = slice(t * part, (t + 1) * part)
            for c, value in enumerate(weights_of(cell(nfield, t), cell(nfield + 1, t), cell(nfield + 2, t))):
                coef_ref[0, c, at] = value
            for c, value in enumerate(weights_of(strip(1, t), strip(2, t), strip(3, t))):
                coef_ref[1, c, at] = value
        for f in range(nfield):
            for t in range(total):
                state_ref[0, f, t * part : (t + 1) * part] = cell(f, t)

        state = {t: strip(0, t) for t in range(total)}
        for step in range(STEPS):
            inner = range(step + 1, total - 1 - step)
            for t in inner:
                narrow = state[t].astype(BF16)
                for f in range(nfield):
                    join_ref[step, f, t * part : (t + 1) * part] = narrow * of_field[f]
            if step < STEPS - 1:
                state = {
                    t: stepped(
                        [coef_ref[1, c, t * part : (t + 1) * part] for c in range(5)],
                        state[t],
                        pltpu.roll(state[t], LANE - 1, 1),
                        pltpu.roll(state[t], 1, 1),
                        state[t + 1],
                        state[t - 1],
                    )
                    for t in inner
                }

        def rows_of(step, by=0):
            return slice((step + 1 + by) * part, (total - 1 - step + by) * part)

        def neighbours(step, pair):
            at = rows_of(step)
            cells = [
                jnp.concatenate([state_ref[step % 2, f, at].astype(BF16), join_ref[step, f, at]], axis=1) for f in pair
            ]
            return mul(jnp.concatenate(cells, axis=0), shift_ref[...])

        turns = [(step, pair) for step in range(STEPS) for pair in ((0, 1), (2, 3))]
        ready = neighbours(*turns[0])
        for turn, (step, pair) in enumerate(turns):
            sides = ready
            if turn + 1 < len(turns):
                ready = neighbours(*turns[turn + 1])
            size = (total - 2 - 2 * step) * part
            cur = step % 2
            for u in range(step + 1, total - 1 - step):
                at, side = slice(u * part, (u + 1) * part), (u - step - 1) * part
                coef = [coef_ref[0, c, at] for c in range(5)]
                for n, f in enumerate(pair):
                    value = stepped(
                        coef,
                        state_ref[cur, f, at],
                        sides[n * size + side : n * size + side + part, :LANE],
                        sides[n * size + side : n * size + side + part, LANE:],
                        state_ref[cur, f, (u + 1) * part : (u + 2) * part],
                        state_ref[cur, f, (u - 1) * part : u * part],
                    )
                    if step < STEPS - 1:
                        state_ref[1 - cur, f, at] = value
                    else:
                        out_ref[f, pl.ds(sub * (part * rows) + u - STEPS, part, stride=rows), :] = value
        return carry

    lax.fori_loop(0, GROUP // part, levels, 0)


class Dynamics:
    def __init__(self, fields, coefs, rows, levels):
        self.args = (fields, *coefs)
        self.rows, self.levels = rows, levels
        nfield = fields.shape[0]
        planes = nfield + len(coefs)
        groups = pl.cdiv(levels, GROUP)
        self.grid = (groups,)
        self.planes = planes
        self.strip_rows = (rows + 2 * STEPS) * GROUP
        self.fields_spec = pl.BlockSpec((nfield, GROUP * rows, LANE), lambda i: (0, i, 0))
        self.arg_specs = [self.fields_spec] + [pl.BlockSpec((GROUP * rows, LANE), lambda i: (i, 0))] * 3
        self.rim_spec = pl.BlockSpec((STEPS, planes, GROUP, LANE), lambda i: (0, 0, i, 0))
        self.rim_shape = jax.ShapeDtypeStruct((STEPS, planes, groups * GROUP, LANE), BF16)
        self.strip_spec = pl.BlockSpec((self.strip_rows, LANE), lambda i: (0, 0))
        self.strip_shape = jax.ShapeDtypeStruct((self.strip_rows, LANE), BF16)

    def rims(self, start):
        def kernel(*refs):
            rim_kernel(*refs, rows=self.rows, levels=self.levels)

        return pl.pallas_call(
            kernel,
            grid=self.grid,
            in_specs=self.arg_specs,
            out_specs=[self.rim_spec, self.rim_spec],
            out_shape=[self.rim_shape, self.rim_shape],
            name="rims",
        )(self.args[0], *after(self.args[1:], start))

    def send_rims(self, low, high):
        size = lax.axis_size("lat")
        up = [(i, i + 1) for i in range(size - 1)]
        south = lax.ppermute(high, "lat", up)
        north = lax.ppermute(low, "lat", [(j, i) for i, j in up])
        return south, north

    def strips(self, south, north, start):
        def kernel(*refs):
            strip_kernel(*refs, rows=self.rows, levels=self.levels)

        south, north = after((south, north), start)
        return pl.pallas_call(
            kernel,
            grid=self.grid,
            in_specs=self.arg_specs + [self.rim_spec, self.rim_spec],
            out_specs=[self.strip_spec, self.strip_spec],
            out_shape=[self.strip_shape, self.strip_shape],
            scratch_shapes=[
                pltpu.VMEM((self.strip_rows, self.planes * LANE), BF16),
                pltpu.VMEM((self.strip_rows, 2 * LANE), F32),
            ],
            name="strips",
        )(*self.args, south, north)

    def send_strips(self, own_w, own_e):
        size = lax.axis_size("lon")
        around = [(i, (i + 1) % size) for i in range(size)]
        from_w = lax.ppermute(own_e, "lon", around)
        from_e = lax.ppermute(own_w, "lon", [(j, i) for i, j in around])
        return from_w, from_e

    def steps(self, first, count, rims, strips, start, state=None):
        def kernel(*refs):
            inputs = refs[:10]
            dynamics_kernel(*inputs, *refs[10 + (state is not None) :], rows=self.rows, first=first)

        fields = self.args[0]
        nfield = fields.shape[0]
        chunk = GROUP * self.rows
        fields_spec = pl.BlockSpec((nfield, chunk, LANE), lambda i: (0, i + first, 0))
        coef_spec = pl.BlockSpec((chunk, LANE), lambda i: (i + first, 0))
        rim_spec = pl.BlockSpec((STEPS, self.planes, GROUP, LANE), lambda i: (0, 0, i + first, 0))
        specs = [fields_spec] + [coef_spec] * 3 + [rim_spec] * 2 + [self.strip_spec] * 4
        operands = self.args + rims + after(strips, start)
        aliases = {}
        if state is not None:
            specs.append(pl.BlockSpec(memory_space=pl.ANY))
            aliases = {len(operands): 0}
            operands += (state,)
        cells = (self.rows + 2 * STEPS) * LEVELS
        return pl.pallas_call(
            kernel,
            grid=(count,),
            in_specs=specs,
            out_specs=fields_spec,
            out_shape=jax.ShapeDtypeStruct(fields.shape, F32),
            input_output_aliases=aliases,
            scratch_shapes=[
                pltpu.VMEM((2, STEPS, self.planes, GROUP, LANE), F32),
                pltpu.VMEM((self.strip_rows, 4 * LANE), F32),
                pltpu.VMEM((2, 5, cells, LANE), F32),
                pltpu.VMEM((STEPS, nfield, cells, LANE), BF16),
                pltpu.VMEM((2, nfield, cells, LANE), F32),
                pltpu.VMEM((2 * LANE, 2 * LANE), BF16),
            ],
            cost_estimate=pl.CostEstimate(
                flops=fields.size * 60 * count // self.grid[0],
                transcendentals=0,
                bytes_accessed=fields.size * 11 * count // self.grid[0],
            ),
            name="dynamics",
        )(*operands)


def after(values, start):
    return lax.optimization_barrier((values, start))[0]


def exchange(array, axis):
    return lax.all_to_all(array, axis, split_axis=0, concat_axis=0, tiled=True)


def spread(piece):
    size = lax.axis_size("lat")
    held = [piece]
    for flip in (1, 2, 4):
        mine = jnp.concatenate(held, axis=0) if len(held) > 1 else held[0]
        theirs = lax.ppermute(mine, "lat", [(i, i ^ flip) for i in range(size)])
        held = [mine, theirs]
        if flip == 2:
            chips = held
    return chips + [theirs]


def scattered(parts, start):
    size = parts.shape[0]
    core = lax.axis_index("lat") % 2
    pairs = parts.reshape((size // 2, 2) + parts.shape[1:])
    mine = lax.dynamic_index_in_dim(pairs, core, 1, keepdims=False)
    other = lax.dynamic_index_in_dim(pairs, 1 - core, 1, keepdims=False)
    other = lax.ppermute(other, "lat", [(i, i ^ 1) for i in range(size)])
    both = mine.astype(F32) + other.astype(F32)
    chips = size // 2
    chip = lax.axis_index("lat") // 2
    total = lax.dynamic_index_in_dim(both, chip, 0, keepdims=False)
    both = after(both.astype(BF16), start)
    for shift in range(1, chips):
        part = lax.dynamic_index_in_dim(both, (chip + shift) % chips, 0, keepdims=False)
        to = [(i, (i + 2 * shift) % size) for i in range(size)]
        total = total + lax.ppermute(part, "lat", to).astype(F32)
    return total


def shards(
    fields,
    courant_lon,
    courant_lat,
    diffusion,
    tend_cot,
    col_list,
    block_count,
    block_dest,
    w_in,
    w_mid,
    w_out,
):
    nfield, levels, rows, columns = fields.shape
    feat = nfield * levels
    hid_mid, hid_own = w_mid.shape[1:]
    nlat = lax.axis_size("lat")
    pad = -feat % LANE
    cuts = (
        (0, feat),
        (feat + pad, feat + pad + hid_mid),
        (feat + pad + hid_mid, 2 * feat + pad + hid_mid),
    )
    span = cuts[2][1] + pad

    coefs = [c.reshape(levels * rows, columns) for c in (courant_lon, courant_lat, diffusion)]
    window = Dynamics(fields.reshape(nfield, levels * rows, columns), coefs, rows, levels)

    nblock = block_dest.shape[-1]
    cols = col_list.reshape(nblock, 1, LANE)
    send_x, table = gather_first(block_dest, block_count, cols, fields.reshape(feat * rows, columns), feat, rows)
    recv_x = exchange(send_x, "lon")
    rest = jnp.zeros((pad, hid_own), BF16)
    own = jnp.concatenate([w_in[0], rest, w_mid[0], w_out[0], rest], axis=0).T
    pieces = spread(after(own, send_x))
    lat = lax.axis_index("lat")
    at = jnp.stack([lat // 2, lat % 2]).astype(jnp.int32)
    low, high = window.rims(send_x)
    south, north = window.send_rims(low, high)
    send_g = gather_columns(after(table, low), tend_cot.reshape(feat * rows, columns), feat, rows)
    recv_g = exchange(send_g, "lon")
    own_w, own_e = window.strips(south, north, send_g)
    from_w, from_e = window.send_strips(own_w, own_e)
    tend, a_one, a_two = physics_forward(at, after(recv_x, own_w), pieces, cuts)
    back_tend = exchange(tend, "lon")
    adj, grads = physics_backward(at, recv_x, recv_g, a_one, a_two, pieces, cuts)
    rims, strips = (south, north), (own_w, own_e, from_e, from_w)
    last = window.grid[0] - 1
    state = window.steps(last, 1, rims, strips, adj)
    back_adj = exchange(after(adj, back_tend), "lon")
    state = window.steps(0, last, rims, strips, back_tend, state)
    summed = scattered(grads.reshape(nlat, hid_own, span), back_tend).T
    grad_in, grad_mid, grad_out = (summed[a:b][None] for a, b in cuts)

    new_fields = scatter_columns(table, back_tend, rows, state.reshape(feat * rows, columns))
    adjoint = scatter_columns(table, back_adj, rows)
    return (new_fields.reshape(fields.shape), adjoint.reshape(fields.shape), grad_in, grad_mid, grad_out)


def solution(mesh):
    return jax.shard_map(
        shards,
        mesh=mesh,
        in_specs=(
            P(None, None, "lat", "lon"),
            P(None, "lat", "lon"),
            P(None, "lat", "lon"),
            P(None, "lat", "lon"),
            P(None, None, "lat", "lon"),
            P("lat", "lon", None),
            P("lat", "lon", None),
            P("lat", "lon", None),
            P("lon", None, "lat"),
            P("lon", None, "lat"),
            P("lon", None, "lat"),
        ),
        out_specs=(
            P(None, None, "lat", "lon"),
            P(None, None, "lat", "lon"),
            P("lon", None, "lat"),
            P("lon", None, "lat"),
            P("lon", None, "lat"),
        ),
        check_vma=False,
    )
```

```python
import jax
import jax.numpy as jnp
from jax import lax
from jax.experimental import pallas as pl
from jax.experimental.pallas import tpu as pltpu
from jax.sharding import PartitionSpec as P


STEPS = 4
LANE = 128
WIDE = 4
GROUP = 32
LEVELS = 16
F32 = jnp.float32
BF16 = jnp.bfloat16


def iota(shape, dim):
    return lax.broadcasted_iota(jnp.int32, shape, dim)


def rows_of_source(src_ref, mat_ref, rows):
    for r in range(rows):
        mat_ref[:, r * LANE : (r + 1) * LANE] = src_ref[pl.ds(r, mat_ref.shape[0], stride=rows), :].astype(BF16)


def gather_blocks(table_ref, mat_ref, out_ref):
    ncol = mat_ref.shape[1]
    first = pl.program_id(0) * WIDE
    column = iota((ncol, LANE), 0)
    hot = [jnp.where(column == table_ref[pl.ds(first + b, 1), :], 1.0, 0.0).astype(BF16) for b in range(WIDE)]
    got = jnp.dot(mat_ref[...], jnp.concatenate(hot, axis=1), preferred_element_type=F32).astype(BF16)
    for b in range(WIDE):
        out_ref[b] = got[:, b * LANE : (b + 1) * LANE]


def gather_first_kernel(dest_ref, count_ref, cols_ref, src_ref, out_ref, table_ref, mat_ref, full_ref, sems, *, rows):
    feat = mat_ref.shape[0]

    @pl.when(pl.program_id(0) == 0)
    def _():
        cuts = [(start, min(start + LANE, feat)) for start in range(0, feat, LANE)]
        loads = []
        for n, (start, stop) in enumerate(cuts):
            at = pl.ds(start * rows, (stop - start) * rows)
            loads.append(pltpu.make_async_copy(src_ref.at[at], full_ref.at[at], sems.at[n]))
            loads[-1].start()
        slot = iota((1, LANE), 1)
        for b in range(cols_ref.shape[0]):
            row = jnp.where(slot < count_ref[0, 0, b], cols_ref[b], -1)
            table_ref[pl.ds(dest_ref[0, 0, b], 1), :] = row
        for load, (start, stop) in zip(loads, cuts):
            load.wait()
            for r in range(rows):
                part = full_ref[pl.ds(start * rows + r, stop - start, stride=rows), :]
                mat_ref[start:stop, r * LANE : (r + 1) * LANE] = part.astype(BF16)

    gather_blocks(table_ref, mat_ref, out_ref)


def gather_kernel(table_ref, src_ref, out_ref, mat_ref, wide_ref, *, rows):
    @pl.when(pl.program_id(0) == 0)
    def _():
        wide_ref[...] = src_ref[...].astype(F32)
        rows_of_source(wide_ref, mat_ref, rows)

    gather_blocks(table_ref, mat_ref, out_ref)


def gather_parts(source, nblock, feat, rows):
    once = pl.BlockSpec(source.shape, lambda i: (0, 0), pipeline_mode=pl.Buffered(1))
    out = pl.BlockSpec((WIDE, feat, LANE), lambda i: (i, 0, 0))
    shape = jax.ShapeDtypeStruct((nblock, feat, LANE), BF16)
    cost = pl.CostEstimate(
        flops=2 * feat * rows * LANE * nblock * LANE,
        transcendentals=0,
        bytes_accessed=source.size * source.dtype.itemsize + feat * nblock * LANE * 2,
    )
    return once, out, shape, cost


def gather_first(dest, count, cols, source, feat, rows):
    nblock = cols.shape[0]
    _, out, shape, cost = gather_parts(source, nblock, feat, rows)
    table = jax.ShapeDtypeStruct((nblock, LANE), jnp.int32)

    def kernel(*refs):
        gather_first_kernel(*refs, rows=rows)

    scalars = pl.BlockSpec(memory_space=pltpu.SMEM)
    return pl.pallas_call(
        kernel,
        grid=(nblock // WIDE,),
        in_specs=[scalars, scalars, pl.BlockSpec(cols.shape, lambda i: (0, 0, 0)), pl.BlockSpec(memory_space=pl.ANY)],
        out_specs=[out, pl.BlockSpec(table.shape, lambda i: (0, 0))],
        out_shape=[shape, table],
        scratch_shapes=[
            pltpu.VMEM((feat, rows * LANE), BF16),
            pltpu.VMEM(source.shape, F32),
            pltpu.SemaphoreType.DMA((pl.cdiv(feat, LANE),)),
        ],
        cost_estimate=cost,
        name="gather_first",
    )(dest, count, cols, source)


def gather_columns(table, source, feat, rows):
    nblock = table.shape[0]
    once, out, shape, cost = gather_parts(source, nblock, feat, rows)

    def kernel(*refs):
        gather_kernel(*refs, rows=rows)

    return pl.pallas_call(
        kernel,
        grid=(nblock // WIDE,),
        in_specs=[pl.BlockSpec(table.shape, lambda i: (0, 0)), once],
        out_specs=out,
        out_shape=shape,
        scratch_shapes=[pltpu.VMEM((feat, rows * LANE), BF16), pltpu.VMEM(source.shape, F32)],
        cost_estimate=cost,
        name="gather_columns",
    )(table, source)


def scatter_rows(table_ref, blocks_ref, mat_ref, where_ref):
    nblock = blocks_ref.shape[0]

    @pl.when(pl.program_id(0) == 0)
    def _():
        table = table_ref[...].astype(F32)
        by_slot = jnp.concatenate([table, jnp.zeros((LANE - nblock, LANE), F32)], axis=0).T
        for b in range(nblock):
            mat_ref[:, b * LANE : (b + 1) * LANE] = blocks_ref[b]
            column = jnp.broadcast_to(by_slot[:, b : b + 1], (LANE, LANE))
            where_ref[b * LANE : (b + 1) * LANE, :] = column.astype(jnp.int32)

    where = where_ref[...]
    lane = iota(where.shape, 1) + pl.program_id(0) * (WIDE * LANE)
    hot = [jnp.where(where == lane + r * LANE, 1.0, 0.0).astype(BF16) for r in range(WIDE)]
    return jnp.dot(mat_ref[...], jnp.concatenate(hot, axis=1), preferred_element_type=F32)


def scatter_add_kernel(table_ref, blocks_ref, base_ref, out_ref, mat_ref, where_ref, *, rows):
    got = scatter_rows(table_ref, blocks_ref, mat_ref, where_ref)
    for r in range(WIDE):
        at = pl.ds(pl.program_id(0) * WIDE + r, mat_ref.shape[0], stride=rows)
        out_ref[at, :] = base_ref[at, :] + got[:, r * LANE : (r + 1) * LANE]


def scatter_kernel(table_ref, blocks_ref, out_ref, mat_ref, where_ref, full_ref, *, rows):
    got = scatter_rows(table_ref, blocks_ref, mat_ref, where_ref)
    for r in range(WIDE):
        at = pl.ds(pl.program_id(0) * WIDE + r, mat_ref.shape[0], stride=rows)
        full_ref[at, :] = got[:, r * LANE : (r + 1) * LANE]

    @pl.when(pl.program_id(0) == pl.num_programs(0) - 1)
    def _():
        out_ref[...] = full_ref[...].astype(BF16)


def scatter_columns(table, blocks, rows, base=None):
    nblock, feat, length = blocks.shape
    nslot = nblock * length
    shape = (feat * rows, LANE)
    whole = pl.BlockSpec(shape, lambda i: (0, 0), pipeline_mode=pl.Buffered(1))
    specs = [
        pl.BlockSpec(table.shape, lambda i: (0, 0)),
        pl.BlockSpec(blocks.shape, lambda i: (0, 0, 0), pipeline_mode=pl.Buffered(1)),
    ]
    scratch = [pltpu.VMEM((feat, nslot), BF16), pltpu.VMEM((nslot, LANE), jnp.int32)]
    if base is None:
        body, operands, dtype = scatter_kernel, (table, blocks), BF16
        scratch.append(pltpu.VMEM(shape, F32))
    else:
        body, operands, dtype = scatter_add_kernel, (table, blocks, base), F32
        specs.append(whole)

    def kernel(*refs):
        body(*refs, rows=rows)

    return pl.pallas_call(
        kernel,
        grid=(rows // WIDE,),
        in_specs=specs,
        out_specs=pl.BlockSpec(shape, lambda i: (0, 0)),
        out_shape=jax.ShapeDtypeStruct(shape, dtype),
        scratch_shapes=scratch,
        cost_estimate=pl.CostEstimate(
            flops=2 * feat * nslot * rows * LANE, transcendentals=0, bytes_accessed=feat * nslot * 8
        ),
        name="scatter_columns",
    )(*operands)


def wide(ref):
    return jnp.concatenate([ref[b] for b in range(ref.shape[0])], axis=1)


def normalised(x):
    xf = x.astype(F32)
    scale = lax.rsqrt(jnp.mean(xf * xf, axis=0, keepdims=True) + 1e-06)
    return xf, scale, (xf * scale).astype(BF16)


def mul(a, b):
    return jnp.dot(a, b, preferred_element_type=F32)


def mul_slots(a, b):
    return lax.dot_general(a, b, (((1,), (1,)), ((), ())), preferred_element_type=F32)


def place_weights(at_ref, piece_refs, w_t_ref, w_ref, parts):
    chips = len(piece_refs)
    size = piece_refs[0].shape[0] // 2
    for n, piece in enumerate(piece_refs):
        chip = (at_ref[0] + (chips - n)) % chips
        for half in range(2):
            core = at_ref[1] if half == 0 else 1 - at_ref[1]
            at = pl.multiple_of((2 * chip + core) * size, size)
            w_t_ref[pl.ds(at, size), :] = piece[half * size : (half + 1) * size, :]
    row = 0
    for start, stop in parts:
        w_ref[row : row + stop - start, :] = w_t_ref[:, start:stop].T
        row += stop - start


def forward_kernel(at_ref, x_ref, *refs, cuts):
    *piece_refs, tend_ref, a1_ref, a2_ref, w_t_ref, w_ref = refs
    (in0, in1), (mid0, mid1), (out0, out1) = cuts

    @pl.when(pl.program_id(0) == 0)
    def _():
        place_weights(at_ref, piece_refs, w_t_ref, w_ref, [(out0, w_t_ref.shape[1])])

    _, _, xn = normalised(wide(x_ref))
    a_one = mul(w_t_ref[:, in0:in1], xn)
    a1_ref[...] = a_one
    h_one = (a_one * jax.nn.sigmoid(a_one)).astype(BF16)
    a_two = mul(w_t_ref[:, mid0:mid1], h_one)
    a2_ref[...] = a_two
    h_two = (a_two * jax.nn.sigmoid(a_two)).astype(BF16)
    tend = mul(w_ref[: out1 - out0, :], h_two).astype(BF16)
    for b in range(x_ref.shape[0]):
        tend_ref[b] = tend[:, b * LANE : (b + 1) * LANE]


def backward_kernel(at_ref, x_ref, g_ref, a1_ref, a2_ref, *refs, cuts):
    *piece_refs, adj_ref, grad_ref, w_t_ref, w_ref, sum_ref = refs
    (in0, in1), (mid0, mid1), (out0, out1) = cuts

    @pl.when(pl.program_id(0) == 0)
    def _():
        place_weights(at_ref, piece_refs, w_t_ref, w_ref, [(0, out0)])
        sum_ref[...] = jnp.zeros_like(sum_ref)

    xf, scale, xn = normalised(wide(x_ref))
    g = wide(g_ref)
    a_two = a2_ref[...]
    sig = jax.nn.sigmoid(a_two)
    h_two = (a_two * sig).astype(BF16)
    d_two = (mul(w_t_ref[:, out0:out1], g) * (sig * (1.0 + a_two * (1.0 - sig)))).astype(BF16)
    sum_ref[:, out0:out1] += mul_slots(h_two, g)
    a_one = a1_ref[...]
    sig = jax.nn.sigmoid(a_one)
    h_one = (a_one * sig).astype(BF16)
    d_one = (mul(w_ref[mid0:mid1, :], d_two) * (sig * (1.0 + a_one * (1.0 - sig)))).astype(BF16)
    sum_ref[:, mid0:mid1] += mul_slots(d_two, h_one)
    d_norm = mul(w_ref[in0:in1, :], d_one)
    adj = (
        scale * d_norm - xf * (scale * scale * scale) * jnp.mean(xf * d_norm, axis=0, keepdims=True)
    ).astype(BF16)
    for b in range(x_ref.shape[0]):
        adj_ref[b] = adj[:, b * LANE : (b + 1) * LANE]
    sum_ref[:, in0:in1] += mul_slots(d_one, xn)

    @pl.when(pl.program_id(0) == pl.num_programs(0) - 1)
    def _():
        grad_ref[...] = sum_ref[...].astype(BF16)


def column_specs(shape, pieces):
    _, feat, length = shape
    rows, span = pieces[0].shape
    hid = rows * len(pieces)
    block = pl.BlockSpec((WIDE, feat, length), lambda i: (i, 0, 0))
    hidden = pl.BlockSpec((hid, WIDE * length), lambda i: (0, i))
    piece = pl.BlockSpec((rows, span), lambda i: (0, 0), pipeline_mode=pl.Buffered(1))
    return hid, span, block, hidden, [piece] * len(pieces)


def physics_forward(at, x, pieces, cuts):
    nblock, feat, length = x.shape
    hid, span, block, hidden, piece_specs = column_specs(x.shape, pieces)

    def kernel(*refs):
        forward_kernel(*refs, cuts=cuts)

    kept = jax.ShapeDtypeStruct((hid, nblock * length), F32)
    return pl.pallas_call(
        kernel,
        grid=(nblock // WIDE,),
        in_specs=[pl.BlockSpec(memory_space=pltpu.SMEM), block] + piece_specs,
        out_specs=[block, hidden, hidden],
        out_shape=[jax.ShapeDtypeStruct(x.shape, BF16), kept, kept],
        scratch_shapes=[pltpu.VMEM((hid, span), BF16), pltpu.VMEM((span - cuts[2][0], hid), BF16)],
        cost_estimate=pl.CostEstimate(
            flops=2 * hid * (2 * feat + hid) * nblock * length,
            transcendentals=4 * hid * nblock * length,
            bytes_accessed=x.size * 4 + hid * nblock * length * 8,
        ),
        name="physics_forward",
    )(at, x, *pieces)


def physics_backward(at, x, g, a_one, a_two, pieces, cuts):
    nblock, feat, length = x.shape
    hid, span, block, hidden, piece_specs = column_specs(x.shape, pieces)

    def kernel(*refs):
        backward_kernel(*refs, cuts=cuts)

    return pl.pallas_call(
        kernel,
        grid=(nblock // WIDE,),
        in_specs=[pl.BlockSpec(memory_space=pltpu.SMEM), block, block, hidden, hidden] + piece_specs,
        out_specs=[block, pl.BlockSpec((hid, span), lambda i: (0, 0))],
        out_shape=[jax.ShapeDtypeStruct(x.shape, BF16), jax.ShapeDtypeStruct((hid, span), BF16)],
        scratch_shapes=[
            pltpu.VMEM((hid, span), BF16),
            pltpu.VMEM((cuts[2][0], hid), BF16),
            pltpu.VMEM((hid, span), F32),
        ],
        cost_estimate=pl.CostEstimate(
            flops=4 * hid * (2 * feat + hid) * nblock * length,
            transcendentals=4 * hid * nblock * length,
            bytes_accessed=x.size * 6 + hid * nblock * length * 8,
        ),
        name="physics_backward",
    )(at, x, g, a_one, a_two, *pieces)


def plane(fields_ref, coef_refs, a, at):
    nfield = fields_ref.shape[0]
    return fields_ref[a, at, :] if a < nfield else coef_refs[a - nfield][at, :]


def inside(levels):
    return iota((GROUP, LANE), 0) + pl.program_id(0) * GROUP < levels


def rim_kernel(fields_ref, lon_ref, lat_ref, dif_ref, low_ref, high_ref, *, rows, levels):
    coefs = (lon_ref, lat_ref, dif_ref)
    keep = inside(levels)
    for r in range(STEPS):
        for a in range(low_ref.shape[1]):
            for first, out in ((r, low_ref), (rows - STEPS + r, high_ref)):
                value = plane(fields_ref, coefs, a, pl.ds(first, GROUP, stride=rows))
                out[r, a] = jnp.where(keep, value, 0.0).astype(BF16)


def strip_kernel(
    fields_ref, lon_ref, lat_ref, dif_ref, south_ref, north_ref, west_ref, east_ref, all_ref, sum_ref, *, rows, levels
):
    coefs = (lon_ref, lat_ref, dif_ref)
    planes = south_ref.shape[1]
    keep = inside(levels)
    for t in range(rows + 2 * STEPS):
        for a in range(planes):
            if t < STEPS:
                value = south_ref[t, a]
            elif t >= rows + STEPS:
                value = north_ref[t - rows - STEPS, a]
            else:
                own = plane(fields_ref, coefs, a, pl.ds(t - STEPS, GROUP, stride=rows))
                value = jnp.where(keep, own, 0.0).astype(BF16)
            all_ref[t * GROUP : (t + 1) * GROUP, a * LANE : (a + 1) * LANE] = value
    shape = (planes * LANE, 2 * LANE)
    k, n = iota(shape, 0), iota(shape, 1)
    a, q = k // LANE, k % LANE
    west = jnp.where(q < STEPS, STEPS * a + q, -1)
    east = jnp.where(q >= LANE - STEPS, STEPS * a + q - (LANE - STEPS) + LANE, -1)
    pick = jnp.where((n == west) | (n == east), 1.0, 0.0).astype(BF16)
    got = jnp.dot(all_ref[...], pick, preferred_element_type=F32)
    group = pl.program_id(0)

    @pl.when(group == 0)
    def _():
        sum_ref[...] = got

    @pl.when(group > 0)
    def _():
        for half in range(2):
            part = got[:, half * LANE : (half + 1) * LANE]
            sum_ref[:, half * LANE : (half + 1) * LANE] += pltpu.roll(part, group * GROUP, 1)

    @pl.when(group == pl.num_programs(0) - 1)
    def _():
        west_ref[...] = sum_ref[:, :LANE].astype(BF16)
        east_ref[...] = sum_ref[:, LANE:].astype(BF16)


def weights_of(c_lon, c_lat, c_dif):
    return (
        1.0 - 4.0 * c_dif,
        c_dif - 0.5 * c_lon,
        c_dif + 0.5 * c_lon,
        c_dif - 0.5 * c_lat,
        c_dif + 0.5 * c_lat,
    )


def stepped(coef, centre, east, west, north, south):
    return coef[0] * centre + (coef[1] * east + coef[2] * west) + (coef[3] * north + coef[4] * south)


def dynamics_kernel(
    fields_ref,
    lon_ref,
    lat_ref,
    dif_ref,
    south_ref,
    north_ref,
    own_w_ref,
    own_e_ref,
    from_e_ref,
    from_w_ref,
    out_ref,
    rim_ref,
    strip_ref,
    coef_ref,
    join_ref,
    state_ref,
    shift_ref,
    *,
    rows,
    first,
):
    coefs = (lon_ref, lat_ref, dif_ref)
    nfield = fields_ref.shape[0]
    total = rows + 2 * STEPS
    rim_ref[0] = south_ref[...].astype(F32)
    rim_ref[1] = north_ref[...].astype(F32)

    @pl.when(pl.program_id(0) % (GROUP // LEVELS) == 0)
    def _():
        sources = jnp.concatenate([own_e_ref[...], from_e_ref[...], from_w_ref[...], own_w_ref[...]], axis=1)
        k = iota((4 * LANE, LANE), 0)
        lane = k % LANE
        row_code = (k // LANE) * STEPS + lane % STEPS + 16 * ((lane // STEPS) % 8)
        row_code = jnp.where(lane // GROUP == pl.program_id(0) // (GROUP // LEVELS) + first, row_code, -1)
        m = iota((1, LANE), 1)
        picks = []
        for kind in range(4):
            col_code = m if kind == 0 else m % 16 + 16 * (nfield - 1 + kind)
            col_code = jnp.where(m < 16 * nfield, col_code, -2)
            picks.append(jnp.where(row_code == col_code, 1.0, 0.0).astype(BF16))
        pick = jnp.concatenate(picks, axis=1)
        strip_ref[...] = jnp.dot(sources, pick, preferred_element_type=F32)

    @pl.when(pl.program_id(0) == 0)
    def _():
        shape = (2 * LANE, 2 * LANE)
        k, n = iota(shape, 0), iota(shape, 1)
        east = jnp.where(k < LANE, k - 1, jnp.where(k % 16 == 4, LANE - 1, -1))
        west = jnp.where(k < LANE - 1, k + 1 + LANE, jnp.where((k >= LANE) & (k % 16 == 11), LANE, -1))
        shift_ref[...] = jnp.where(((n == east) & (k > 0)) | (n == west), 1.0, 0.0).astype(BF16)

    part = LEVELS
    lane = iota((part, LANE), 1)
    of_field = [jnp.where(lane // 16 == f, 1.0, 0.0).astype(BF16) for f in range(nfield)]

    sub = pl.program_id(0) % (GROUP // part)

    def levels():
        def cell(a, t):
            if STEPS <= t < rows + STEPS:
                return plane(fields_ref, coefs, a, pl.ds(t - STEPS, part, stride=rows))
            side, at = (0, t) if t < STEPS else (1, t - rows - STEPS)
            return rim_ref[side, at, a]

        def strip(kind, t):
            return strip_ref[pl.ds(t * GROUP + sub * part, part), kind * LANE : (kind + 1) * LANE]

        for t in range(1, total - 1):
            at = slice(t * part, (t + 1) * part)
            for c, value in enumerate(weights_of(cell(nfield, t), cell(nfield + 1, t), cell(nfield + 2, t))):
                coef_ref[0, c, at] = value
            for c, value in enumerate(weights_of(strip(1, t), strip(2, t), strip(3, t))):
                coef_ref[1, c, at] = value
        for f in range(nfield):
            for t in range(total):
                state_ref[0, f, t * part : (t + 1) * part] = cell(f, t)

        state = {t: strip(0, t) for t in range(total)}
        for step in range(STEPS):
            inner = range(step + 1, total - 1 - step)
            for t in inner:
                narrow = state[t].astype(BF16)
                for f in range(nfield):
                    join_ref[step, f, t * part : (t + 1) * part] = narrow * of_field[f]
            if step < STEPS - 1:
                state = {
                    t: stepped(
                        [coef_ref[1, c, t * part : (t + 1) * part] for c in range(5)],
                        state[t],
                        pltpu.roll(state[t], LANE - 1, 1),
                        pltpu.roll(state[t], 1, 1),
                        state[t + 1],
                        state[t - 1],
                    )
                    for t in inner
                }

        def rows_of(step, by=0):
            return slice((step + 1 + by) * part, (total - 1 - step + by) * part)

        def neighbours(step, pair):
            at = rows_of(step)
            cells = [
                jnp.concatenate([state_ref[step % 2, f, at].astype(BF16), join_ref[step, f, at]], axis=1) for f in pair
            ]
            return mul(jnp.concatenate(cells, axis=0), shift_ref[...])

        turns = [(step, pair) for step in range(STEPS) for pair in ((0, 1), (2, 3))]
        ready = neighbours(*turns[0])
        for turn, (step, pair) in enumerate(turns):
            sides = ready
            if turn + 1 < len(turns):
                ready = neighbours(*turns[turn + 1])
            size = (total - 2 - 2 * step) * part
            cur = step % 2
            for u in range(step + 1, total - 1 - step):
                at, side = slice(u * part, (u + 1) * part), (u - step - 1) * part
                coef = [coef_ref[0, c, at] for c in range(5)]
                for n, f in enumerate(pair):
                    value = stepped(
                        coef,
                        state_ref[cur, f, at],
                        sides[n * size + side : n * size + side + part, :LANE],
                        sides[n * size + side : n * size + side + part, LANE:],
                        state_ref[cur, f, (u + 1) * part : (u + 2) * part],
                        state_ref[cur, f, (u - 1) * part : u * part],
                    )
                    if step < STEPS - 1:
                        state_ref[1 - cur, f, at] = value
                    else:
                        out_ref[f, pl.ds(u - STEPS, part, stride=rows), :] = value

    levels()


class Dynamics:
    def __init__(self, fields, coefs, rows, levels):
        self.args = (fields, *coefs)
        self.rows, self.levels = rows, levels
        nfield = fields.shape[0]
        planes = nfield + len(coefs)
        groups = pl.cdiv(levels, GROUP)
        self.grid = (groups,)
        self.planes = planes
        self.strip_rows = (rows + 2 * STEPS) * GROUP
        self.fields_spec = pl.BlockSpec((nfield, GROUP * rows, LANE), lambda i: (0, i, 0))
        self.arg_specs = [self.fields_spec] + [pl.BlockSpec((GROUP * rows, LANE), lambda i: (i, 0))] * 3
        self.rim_spec = pl.BlockSpec((STEPS, planes, GROUP, LANE), lambda i: (0, 0, i, 0))
        self.rim_shape = jax.ShapeDtypeStruct((STEPS, planes, groups * GROUP, LANE), BF16)
        self.strip_spec = pl.BlockSpec((self.strip_rows, LANE), lambda i: (0, 0))
        self.strip_shape = jax.ShapeDtypeStruct((self.strip_rows, LANE), BF16)

    def rims(self, start):
        def kernel(*refs):
            rim_kernel(*refs, rows=self.rows, levels=self.levels)

        return pl.pallas_call(
            kernel,
            grid=self.grid,
            in_specs=self.arg_specs,
            out_specs=[self.rim_spec, self.rim_spec],
            out_shape=[self.rim_shape, self.rim_shape],
            name="rims",
        )(self.args[0], *after(self.args[1:], start))

    def send_rims(self, low, high):
        size = lax.axis_size("lat")
        up = [(i, i + 1) for i in range(size - 1)]
        south = lax.ppermute(high, "lat", up)
        north = lax.ppermute(low, "lat", [(j, i) for i, j in up])
        return south, north

    def strips(self, south, north, start):
        def kernel(*refs):
            strip_kernel(*refs, rows=self.rows, levels=self.levels)

        south, north = after((south, north), start)
        return pl.pallas_call(
            kernel,
            grid=self.grid,
            in_specs=self.arg_specs + [self.rim_spec, self.rim_spec],
            out_specs=[self.strip_spec, self.strip_spec],
            out_shape=[self.strip_shape, self.strip_shape],
            scratch_shapes=[
                pltpu.VMEM((self.strip_rows, self.planes * LANE), BF16),
                pltpu.VMEM((self.strip_rows, 2 * LANE), F32),
            ],
            name="strips",
        )(*self.args, south, north)

    def send_strips(self, own_w, own_e):
        size = lax.axis_size("lon")
        around = [(i, (i + 1) % size) for i in range(size)]
        from_w = lax.ppermute(own_e, "lon", around)
        from_e = lax.ppermute(own_w, "lon", [(j, i) for i, j in around])
        return from_w, from_e

    def steps(self, first, count, rims, strips, start, state=None):
        def kernel(*refs):
            inputs = refs[:10]
            dynamics_kernel(*inputs, *refs[10 + (state is not None) :], rows=self.rows, first=first)

        fields = self.args[0]
        nfield = fields.shape[0]
        chunk = LEVELS * self.rows
        skip = first * (GROUP // LEVELS)
        fields_spec = pl.BlockSpec((nfield, chunk, LANE), lambda i: (0, i + skip, 0))
        coef_spec = pl.BlockSpec((chunk, LANE), lambda i: (i + skip, 0))
        rim_spec = pl.BlockSpec((STEPS, self.planes, LEVELS, LANE), lambda i: (0, 0, i + skip, 0))
        specs = [fields_spec] + [coef_spec] * 3 + [rim_spec] * 2 + [self.strip_spec] * 4
        operands = self.args + rims + after(strips, start)
        aliases = {}
        if state is not None:
            specs.append(pl.BlockSpec(memory_space=pl.ANY))
            aliases = {len(operands): 0}
            operands += (state,)
        cells = (self.rows + 2 * STEPS) * LEVELS
        return pl.pallas_call(
            kernel,
            grid=(count * (GROUP // LEVELS),),
            in_specs=specs,
            out_specs=fields_spec,
            out_shape=jax.ShapeDtypeStruct(fields.shape, F32),
            input_output_aliases=aliases,
            scratch_shapes=[
                pltpu.VMEM((2, STEPS, self.planes, LEVELS, LANE), F32),
                pltpu.VMEM((self.strip_rows, 4 * LANE), F32),
                pltpu.VMEM((2, 5, cells, LANE), F32),
                pltpu.VMEM((STEPS, nfield, cells, LANE), BF16),
                pltpu.VMEM((2, nfield, cells, LANE), F32),
                pltpu.VMEM((2 * LANE, 2 * LANE), BF16),
            ],
            cost_estimate=pl.CostEstimate(
                flops=fields.size * 60 * count // self.grid[0],
                transcendentals=0,
                bytes_accessed=fields.size * 11 * count // self.grid[0],
            ),
            name="dynamics",
        )(*operands)


def after(values, start):
    return lax.optimization_barrier((values, start))[0]


def exchange(array, axis):
    return lax.all_to_all(array, axis, split_axis=0, concat_axis=0, tiled=True)


def spread(piece):
    size = lax.axis_size("lat")
    other = lax.ppermute(piece, "lat", [(i, i ^ 1) for i in range(size)])
    both = jnp.concatenate([piece, other], axis=0)
    pieces = [both]
    for shift in range(1, size // 2):
        pieces.append(lax.ppermute(both, "lat", [(i, (i + 2 * shift) % size) for i in range(size)]))
    return pieces


def scattered(parts, start):
    size = parts.shape[0]
    core = lax.axis_index("lat") % 2
    pairs = parts.reshape((size // 2, 2) + parts.shape[1:])
    mine = lax.dynamic_index_in_dim(pairs, core, 1, keepdims=False)
    other = lax.dynamic_index_in_dim(pairs, 1 - core, 1, keepdims=False)
    other = lax.ppermute(other, "lat", [(i, i ^ 1) for i in range(size)])
    both = mine.astype(F32) + other.astype(F32)
    chips = size // 2
    chip = lax.axis_index("lat") // 2
    total = lax.dynamic_index_in_dim(both, chip, 0, keepdims=False)
    both = after(both.astype(BF16), start)
    for shift in range(1, chips):
        part = lax.dynamic_index_in_dim(both, (chip + shift) % chips, 0, keepdims=False)
        to = [(i, (i + 2 * shift) % size) for i in range(size)]
        total = total + lax.ppermute(part, "lat", to).astype(F32)
    return total


def shards(
    fields,
    courant_lon,
    courant_lat,
    diffusion,
    tend_cot,
    col_list,
    block_count,
    block_dest,
    w_in,
    w_mid,
    w_out,
):
    nfield, levels, rows, columns = fields.shape
    feat = nfield * levels
    hid_mid, hid_own = w_mid.shape[1:]
    nlat = lax.axis_size("lat")
    pad = -feat % LANE
    cuts = (
        (0, feat),
        (feat + pad, feat + pad + hid_mid),
        (feat + pad + hid_mid, 2 * feat + pad + hid_mid),
    )
    span = cuts[2][1] + pad

    coefs = [c.reshape(levels * rows, columns) for c in (courant_lon, courant_lat, diffusion)]
    window = Dynamics(fields.reshape(nfield, levels * rows, columns), coefs, rows, levels)

    nblock = block_dest.shape[-1]
    cols = col_list.reshape(nblock, 1, LANE)
    send_x, table = gather_first(block_dest, block_count, cols, fields.reshape(feat * rows, columns), feat, rows)
    recv_x = exchange(send_x, "lon")
    rest = jnp.zeros((pad, hid_own), BF16)
    own = jnp.concatenate([w_in[0], rest, w_mid[0], w_out[0], rest], axis=0).T
    pieces = spread(after(own, send_x))
    lat = lax.axis_index("lat")
    at = jnp.stack([lat // 2, lat % 2]).astype(jnp.int32)
    low, high = window.rims(send_x)
    south, north = window.send_rims(low, high)
    send_g = gather_columns(after(table, low), tend_cot.reshape(feat * rows, columns), feat, rows)
    recv_g = exchange(send_g, "lon")
    own_w, own_e = window.strips(south, north, send_g)
    from_w, from_e = window.send_strips(own_w, own_e)
    tend, a_one, a_two = physics_forward(at, after(recv_x, own_w), pieces, cuts)
    back_tend = exchange(tend, "lon")
    adj, grads = physics_backward(at, recv_x, recv_g, a_one, a_two, pieces, cuts)
    rims, strips = (south, north), (own_w, own_e, from_e, from_w)
    last = window.grid[0] - 1
    state = window.steps(last, 1, rims, strips, adj)
    back_adj = exchange(after(adj, back_tend), "lon")
    state = window.steps(0, last, rims, strips, back_tend, state)
    summed = scattered(grads.reshape(nlat, hid_own, span), back_tend).T
    grad_in, grad_mid, grad_out = (summed[a:b][None] for a, b in cuts)

    new_fields = scatter_columns(table, back_tend, rows, state.reshape(feat * rows, columns))
    adjoint = scatter_columns(table, back_adj, rows)
    return (new_fields.reshape(fields.shape), adjoint.reshape(fields.shape), grad_in, grad_mid, grad_out)


def solution(mesh):
    return jax.shard_map(
        shards,
        mesh=mesh,
        in_specs=(
            P(None, None, "lat", "lon"),
            P(None, "lat", "lon"),
            P(None, "lat", "lon"),
            P(None, "lat", "lon"),
            P(None, None, "lat", "lon"),
            P("lat", "lon", None),
            P("lat", "lon", None),
            P("lat", "lon", None),
            P("lon", None, "lat"),
            P("lon", None, "lat"),
            P("lon", None, "lat"),
        ),
        out_specs=(
            P(None, None, "lat", "lon"),
            P(None, None, "lat", "lon"),
            P("lon", None, "lat"),
            P("lon", None, "lat"),
            P("lon", None, "lat"),
        ),
        check_vma=False,
    )
```

```python
import jax
import jax.numpy as jnp
from jax import lax
from jax.experimental import pallas as pl
from jax.experimental.pallas import tpu as pltpu
from jax.sharding import PartitionSpec as P


STEPS = 4
LANE = 128
SPAN = 8
WIDE = 4
GROUP = 32
LEVELS = 16
F32 = jnp.float32
BF16 = jnp.bfloat16


def iota(shape, dim):
    return lax.broadcasted_iota(jnp.int32, shape, dim)


def rows_of_source(src_ref, mat_ref, rows):
    for r in range(rows):
        mat_ref[:, r * LANE : (r + 1) * LANE] = src_ref[pl.ds(r, mat_ref.shape[0], stride=rows), :].astype(BF16)


def gather_blocks(table_ref, mat_ref, out_ref):
    ncol = mat_ref.shape[1]
    first = pl.program_id(0) * SPAN
    column = iota((ncol, LANE), 0)
    hot = [jnp.where(column == table_ref[pl.ds(first + b, 1), :], 1.0, 0.0).astype(BF16) for b in range(SPAN)]
    got = jnp.dot(mat_ref[...], jnp.concatenate(hot, axis=1), preferred_element_type=F32).astype(BF16)
    for b in range(SPAN):
        out_ref[b] = got[:, b * LANE : (b + 1) * LANE]


def gather_first_kernel(dest_ref, count_ref, cols_ref, src_ref, out_ref, table_ref, mat_ref, full_ref, sems, *, rows):
    feat = mat_ref.shape[0]

    @pl.when(pl.program_id(0) == 0)
    def _():
        cuts = [(start, min(start + LANE, feat)) for start in range(0, feat, LANE)]
        loads = []
        for n, (start, stop) in enumerate(cuts):
            at = pl.ds(start * rows, (stop - start) * rows)
            loads.append(pltpu.make_async_copy(src_ref.at[at], full_ref.at[at], sems.at[n]))
            loads[-1].start()
        slot = iota((1, LANE), 1)
        for b in range(cols_ref.shape[0]):
            row = jnp.where(slot < count_ref[0, 0, b], cols_ref[b], -1)
            table_ref[pl.ds(dest_ref[0, 0, b], 1), :] = row
        for load, (start, stop) in zip(loads, cuts):
            load.wait()
            for r in range(rows):
                part = full_ref[pl.ds(start * rows + r, stop - start, stride=rows), :]
                mat_ref[start:stop, r * LANE : (r + 1) * LANE] = part.astype(BF16)

    gather_blocks(table_ref, mat_ref, out_ref)


def gather_kernel(table_ref, src_ref, out_ref, mat_ref, wide_ref, *, rows):
    @pl.when(pl.program_id(0) == 0)
    def _():
        wide_ref[...] = src_ref[...].astype(F32)
        rows_of_source(wide_ref, mat_ref, rows)

    gather_blocks(table_ref, mat_ref, out_ref)


def gather_parts(source, nblock, feat, rows):
    once = pl.BlockSpec(source.shape, lambda i: (0, 0), pipeline_mode=pl.Buffered(1))
    out = pl.BlockSpec((SPAN, feat, LANE), lambda i: (i, 0, 0))
    shape = jax.ShapeDtypeStruct((nblock, feat, LANE), BF16)
    cost = pl.CostEstimate(
        flops=2 * feat * rows * LANE * nblock * LANE,
        transcendentals=0,
        bytes_accessed=source.size * source.dtype.itemsize + feat * nblock * LANE * 2,
    )
    return once, out, shape, cost


def gather_first(dest, count, cols, source, feat, rows):
    nblock = cols.shape[0]
    _, out, shape, cost = gather_parts(source, nblock, feat, rows)
    table = jax.ShapeDtypeStruct((nblock, LANE), jnp.int32)

    def kernel(*refs):
        gather_first_kernel(*refs, rows=rows)

    scalars = pl.BlockSpec(memory_space=pltpu.SMEM)
    return pl.pallas_call(
        kernel,
        grid=(nblock // SPAN,),
        in_specs=[scalars, scalars, pl.BlockSpec(cols.shape, lambda i: (0, 0, 0)), pl.BlockSpec(memory_space=pl.ANY)],
        out_specs=[out, pl.BlockSpec(table.shape, lambda i: (0, 0))],
        out_shape=[shape, table],
        scratch_shapes=[
            pltpu.VMEM((feat, rows * LANE), BF16),
            pltpu.VMEM(source.shape, F32),
            pltpu.SemaphoreType.DMA((pl.cdiv(feat, LANE),)),
        ],
        cost_estimate=cost,
        name="gather_first",
    )(dest, count, cols, source)


def gather_columns(table, source, feat, rows):
    nblock = table.shape[0]
    once, out, shape, cost = gather_parts(source, nblock, feat, rows)

    def kernel(*refs):
        gather_kernel(*refs, rows=rows)

    return pl.pallas_call(
        kernel,
        grid=(nblock // SPAN,),
        in_specs=[pl.BlockSpec(table.shape, lambda i: (0, 0)), once],
        out_specs=out,
        out_shape=shape,
        scratch_shapes=[pltpu.VMEM((feat, rows * LANE), BF16), pltpu.VMEM(source.shape, F32)],
        cost_estimate=cost,
        name="gather_columns",
    )(table, source)


def scatter_rows(table_ref, blocks_ref, mat_ref, where_ref):
    nblock = blocks_ref.shape[0]

    @pl.when(pl.program_id(0) == 0)
    def _():
        table = table_ref[...].astype(F32)
        by_slot = jnp.concatenate([table, jnp.zeros((LANE - nblock, LANE), F32)], axis=0).T
        for b in range(nblock):
            mat_ref[:, b * LANE : (b + 1) * LANE] = blocks_ref[b]
            column = jnp.broadcast_to(by_slot[:, b : b + 1], (LANE, LANE))
            where_ref[b * LANE : (b + 1) * LANE, :] = column.astype(jnp.int32)

    where = where_ref[...]
    lane = iota(where.shape, 1) + pl.program_id(0) * (SPAN * LANE)
    hot = [jnp.where(where == lane + r * LANE, 1.0, 0.0).astype(BF16) for r in range(SPAN)]
    return jnp.dot(mat_ref[...], jnp.concatenate(hot, axis=1), preferred_element_type=F32)


def scatter_add_kernel(table_ref, blocks_ref, base_ref, out_ref, mat_ref, where_ref, *, rows):
    got = scatter_rows(table_ref, blocks_ref, mat_ref, where_ref)
    for r in range(SPAN):
        at = pl.ds(pl.program_id(0) * SPAN + r, mat_ref.shape[0], stride=rows)
        out_ref[at, :] = base_ref[at, :] + got[:, r * LANE : (r + 1) * LANE]


def scatter_kernel(table_ref, blocks_ref, out_ref, mat_ref, where_ref, full_ref, *, rows):
    got = scatter_rows(table_ref, blocks_ref, mat_ref, where_ref)
    for r in range(SPAN):
        at = pl.ds(pl.program_id(0) * SPAN + r, mat_ref.shape[0], stride=rows)
        full_ref[at, :] = got[:, r * LANE : (r + 1) * LANE]

    @pl.when(pl.program_id(0) == pl.num_programs(0) - 1)
    def _():
        out_ref[...] = full_ref[...].astype(BF16)


def scatter_columns(table, blocks, rows, base=None):
    nblock, feat, length = blocks.shape
    nslot = nblock * length
    shape = (feat * rows, LANE)
    whole = pl.BlockSpec(shape, lambda i: (0, 0), pipeline_mode=pl.Buffered(1))
    specs = [
        pl.BlockSpec(table.shape, lambda i: (0, 0)),
        pl.BlockSpec(blocks.shape, lambda i: (0, 0, 0), pipeline_mode=pl.Buffered(1)),
    ]
    scratch = [pltpu.VMEM((feat, nslot), BF16), pltpu.VMEM((nslot, LANE), jnp.int32)]
    if base is None:
        body, operands, dtype = scatter_kernel, (table, blocks), BF16
        scratch.append(pltpu.VMEM(shape, F32))
    else:
        body, operands, dtype = scatter_add_kernel, (table, blocks, base), F32
        specs.append(whole)

    def kernel(*refs):
        body(*refs, rows=rows)

    return pl.pallas_call(
        kernel,
        grid=(rows // SPAN,),
        in_specs=specs,
        out_specs=pl.BlockSpec(shape, lambda i: (0, 0)),
        out_shape=jax.ShapeDtypeStruct(shape, dtype),
        scratch_shapes=scratch,
        cost_estimate=pl.CostEstimate(
            flops=2 * feat * nslot * rows * LANE, transcendentals=0, bytes_accessed=feat * nslot * 8
        ),
        name="scatter_columns",
    )(*operands)


def wide(ref):
    return jnp.concatenate([ref[b] for b in range(ref.shape[0])], axis=1)


def normalised(x):
    xf = x.astype(F32)
    scale = lax.rsqrt(jnp.mean(xf * xf, axis=0, keepdims=True) + 1e-06)
    return xf, scale, (xf * scale).astype(BF16)


def mul(a, b):
    return jnp.dot(a, b, preferred_element_type=F32)


def mul_slots(a, b):
    return lax.dot_general(a, b, (((1,), (1,)), ((), ())), preferred_element_type=F32)


def place_weights(at_ref, piece_refs, w_t_ref, w_ref, parts):
    chips = len(piece_refs)
    size = piece_refs[0].shape[0] // 2
    for n, piece in enumerate(piece_refs):
        chip = (at_ref[0] + (chips - n)) % chips
        for half in range(2):
            core = at_ref[1] if half == 0 else 1 - at_ref[1]
            at = pl.multiple_of((2 * chip + core) * size, size)
            w_t_ref[pl.ds(at, size), :] = piece[half * size : (half + 1) * size, :]
    row = 0
    for start, stop in parts:
        w_ref[row : row + stop - start, :] = w_t_ref[:, start:stop].T
        row += stop - start


def forward_kernel(at_ref, x_ref, *refs, cuts):
    *piece_refs, tend_ref, a1_ref, a2_ref, w_t_ref, w_ref = refs
    (in0, in1), (mid0, mid1), (out0, out1) = cuts

    @pl.when(pl.program_id(0) == 0)
    def _():
        place_weights(at_ref, piece_refs, w_t_ref, w_ref, [(out0, w_t_ref.shape[1])])

    _, _, xn = normalised(wide(x_ref))
    a_one = mul(w_t_ref[:, in0:in1], xn)
    a1_ref[...] = a_one
    h_one = (a_one * jax.nn.sigmoid(a_one)).astype(BF16)
    a_two = mul(w_t_ref[:, mid0:mid1], h_one)
    a2_ref[...] = a_two
    h_two = (a_two * jax.nn.sigmoid(a_two)).astype(BF16)
    tend = mul(w_ref[: out1 - out0, :], h_two).astype(BF16)
    for b in range(x_ref.shape[0]):
        tend_ref[b] = tend[:, b * LANE : (b + 1) * LANE]


def backward_kernel(at_ref, x_ref, g_ref, a1_ref, a2_ref, *refs, cuts):
    *piece_refs, adj_ref, grad_ref, w_t_ref, w_ref, sum_ref = refs
    (in0, in1), (mid0, mid1), (out0, out1) = cuts

    @pl.when(pl.program_id(0) == 0)
    def _():
        place_weights(at_ref, piece_refs, w_t_ref, w_ref, [(0, out0)])
        sum_ref[...] = jnp.zeros_like(sum_ref)

    xf, scale, xn = normalised(wide(x_ref))
    g = wide(g_ref)
    a_two = a2_ref[...]
    sig = jax.nn.sigmoid(a_two)
    h_two = (a_two * sig).astype(BF16)
    d_two = (mul(w_t_ref[:, out0:out1], g) * (sig * (1.0 + a_two * (1.0 - sig)))).astype(BF16)
    sum_ref[:, out0:out1] += mul_slots(h_two, g)
    a_one = a1_ref[...]
    sig = jax.nn.sigmoid(a_one)
    h_one = (a_one * sig).astype(BF16)
    d_one = (mul(w_ref[mid0:mid1, :], d_two) * (sig * (1.0 + a_one * (1.0 - sig)))).astype(BF16)
    sum_ref[:, mid0:mid1] += mul_slots(d_two, h_one)
    d_norm = mul(w_ref[in0:in1, :], d_one)
    adj = (
        scale * d_norm - xf * (scale * scale * scale) * jnp.mean(xf * d_norm, axis=0, keepdims=True)
    ).astype(BF16)
    for b in range(x_ref.shape[0]):
        adj_ref[b] = adj[:, b * LANE : (b + 1) * LANE]
    sum_ref[:, in0:in1] += mul_slots(d_one, xn)

    @pl.when(pl.program_id(0) == pl.num_programs(0) - 1)
    def _():
        grad_ref[...] = sum_ref[...].astype(BF16)


def column_specs(shape, pieces):
    _, feat, length = shape
    rows, span = pieces[0].shape
    hid = rows * len(pieces)
    block = pl.BlockSpec((WIDE, feat, length), lambda i: (i, 0, 0))
    hidden = pl.BlockSpec((hid, WIDE * length), lambda i: (0, i))
    piece = pl.BlockSpec((rows, span), lambda i: (0, 0), pipeline_mode=pl.Buffered(1))
    return hid, span, block, hidden, [piece] * len(pieces)


def physics_forward(at, x, pieces, cuts):
    nblock, feat, length = x.shape
    hid, span, block, hidden, piece_specs = column_specs(x.shape, pieces)

    def kernel(*refs):
        forward_kernel(*refs, cuts=cuts)

    kept = jax.ShapeDtypeStruct((hid, nblock * length), F32)
    return pl.pallas_call(
        kernel,
        grid=(nblock // WIDE,),
        in_specs=[pl.BlockSpec(memory_space=pltpu.SMEM), block] + piece_specs,
        out_specs=[block, hidden, hidden],
        out_shape=[jax.ShapeDtypeStruct(x.shape, BF16), kept, kept],
        scratch_shapes=[pltpu.VMEM((hid, span), BF16), pltpu.VMEM((span - cuts[2][0], hid), BF16)],
        cost_estimate=pl.CostEstimate(
            flops=2 * hid * (2 * feat + hid) * nblock * length,
            transcendentals=4 * hid * nblock * length,
            bytes_accessed=x.size * 4 + hid * nblock * length * 8,
        ),
        name="physics_forward",
    )(at, x, *pieces)


def physics_backward(at, x, g, a_one, a_two, pieces, cuts):
    nblock, feat, length = x.shape
    hid, span, block, hidden, piece_specs = column_specs(x.shape, pieces)

    def kernel(*refs):
        backward_kernel(*refs, cuts=cuts)

    return pl.pallas_call(
        kernel,
        grid=(nblock // WIDE,),
        in_specs=[pl.BlockSpec(memory_space=pltpu.SMEM), block, block, hidden, hidden] + piece_specs,
        out_specs=[block, pl.BlockSpec((hid, span), lambda i: (0, 0))],
        out_shape=[jax.ShapeDtypeStruct(x.shape, BF16), jax.ShapeDtypeStruct((hid, span), BF16)],
        scratch_shapes=[
            pltpu.VMEM((hid, span), BF16),
            pltpu.VMEM((cuts[2][0], hid), BF16),
            pltpu.VMEM((hid, span), F32),
        ],
        cost_estimate=pl.CostEstimate(
            flops=4 * hid * (2 * feat + hid) * nblock * length,
            transcendentals=4 * hid * nblock * length,
            bytes_accessed=x.size * 6 + hid * nblock * length * 8,
        ),
        name="physics_backward",
    )(at, x, g, a_one, a_two, *pieces)


def plane(fields_ref, coef_refs, a, at):
    nfield = fields_ref.shape[0]
    return fields_ref[a, at, :] if a < nfield else coef_refs[a - nfield][at, :]


def inside(levels):
    return iota((GROUP, LANE), 0) + pl.program_id(0) * GROUP < levels


def rim_kernel(fields_ref, lon_ref, lat_ref, dif_ref, low_ref, high_ref, *, rows, levels):
    coefs = (lon_ref, lat_ref, dif_ref)
    keep = inside(levels)
    for r in range(STEPS):
        for a in range(low_ref.shape[1]):
            for first, out in ((r, low_ref), (rows - STEPS + r, high_ref)):
                value = plane(fields_ref, coefs, a, pl.ds(first, GROUP, stride=rows))
                out[r, a] = jnp.where(keep, value, 0.0).astype(BF16)


def strip_kernel(
    fields_ref, lon_ref, lat_ref, dif_ref, south_ref, north_ref, west_ref, east_ref, all_ref, sum_ref, *, rows, levels
):
    coefs = (lon_ref, lat_ref, dif_ref)
    planes = south_ref.shape[1]
    keep = inside(levels)
    for t in range(rows + 2 * STEPS):
        for a in range(planes):
            if t < STEPS:
                value = south_ref[t, a]
            elif t >= rows + STEPS:
                value = north_ref[t - rows - STEPS, a]
            else:
                own = plane(fields_ref, coefs, a, pl.ds(t - STEPS, GROUP, stride=rows))
                value = jnp.where(keep, own, 0.0).astype(BF16)
            all_ref[t * GROUP : (t + 1) * GROUP, a * LANE : (a + 1) * LANE] = value
    shape = (planes * LANE, 2 * LANE)
    k, n = iota(shape, 0), iota(shape, 1)
    a, q = k // LANE, k % LANE
    west = jnp.where(q < STEPS, STEPS * a + q, -1)
    east = jnp.where(q >= LANE - STEPS, STEPS * a + q - (LANE - STEPS) + LANE, -1)
    pick = jnp.where((n == west) | (n == east), 1.0, 0.0).astype(BF16)
    got = jnp.dot(all_ref[...], pick, preferred_element_type=F32)
    group = pl.program_id(0)

    @pl.when(group == 0)
    def _():
        sum_ref[...] = got

    @pl.when(group > 0)
    def _():
        for half in range(2):
            part = got[:, half * LANE : (half + 1) * LANE]
            sum_ref[:, half * LANE : (half + 1) * LANE] += pltpu.roll(part, group * GROUP, 1)

    @pl.when(group == pl.num_programs(0) - 1)
    def _():
        west_ref[...] = sum_ref[:, :LANE].astype(BF16)
        east_ref[...] = sum_ref[:, LANE:].astype(BF16)


def weights_of(c_lon, c_lat, c_dif):
    return (
        1.0 - 4.0 * c_dif,
        c_dif - 0.5 * c_lon,
        c_dif + 0.5 * c_lon,
        c_dif - 0.5 * c_lat,
        c_dif + 0.5 * c_lat,
    )


def stepped(coef, centre, east, west, north, south):
    return coef[0] * centre + (coef[1] * east + coef[2] * west) + (coef[3] * north + coef[4] * south)


def dynamics_kernel(
    fields_ref,
    lon_ref,
    lat_ref,
    dif_ref,
    south_ref,
    north_ref,
    own_w_ref,
    own_e_ref,
    from_e_ref,
    from_w_ref,
    out_ref,
    rim_ref,
    strip_ref,
    coef_ref,
    join_ref,
    state_ref,
    shift_ref,
    *,
    rows,
    first,
):
    coefs = (lon_ref, lat_ref, dif_ref)
    nfield = fields_ref.shape[0]
    total = rows + 2 * STEPS
    rim_ref[0] = south_ref[...].astype(F32)
    rim_ref[1] = north_ref[...].astype(F32)

    @pl.when(pl.program_id(0) % (GROUP // LEVELS) == 0)
    def _():
        sources = jnp.concatenate([own_e_ref[...], from_e_ref[...], from_w_ref[...], own_w_ref[...]], axis=1)
        k = iota((4 * LANE, LANE), 0)
        lane = k % LANE
        row_code = (k // LANE) * STEPS + lane % STEPS + 16 * ((lane // STEPS) % 8)
        row_code = jnp.where(lane // GROUP == pl.program_id(0) // (GROUP // LEVELS) + first, row_code, -1)
        m = iota((1, LANE), 1)
        picks = []
        for kind in range(4):
            col_code = m if kind == 0 else m % 16 + 16 * (nfield - 1 + kind)
            col_code = jnp.where(m < 16 * nfield, col_code, -2)
            picks.append(jnp.where(row_code == col_code, 1.0, 0.0).astype(BF16))
        pick = jnp.concatenate(picks, axis=1)
        strip_ref[...] = jnp.dot(sources, pick, preferred_element_type=F32)

    @pl.when(pl.program_id(0) == 0)
    def _():
        shape = (2 * LANE, 2 * LANE)
        k, n = iota(shape, 0), iota(shape, 1)
        east = jnp.where(k < LANE, k - 1, jnp.where(k % 16 == 4, LANE - 1, -1))
        west = jnp.where(k < LANE - 1, k + 1 + LANE, jnp.where((k >= LANE) & (k % 16 == 11), LANE, -1))
        shift_ref[...] = jnp.where(((n == east) & (k > 0)) | (n == west), 1.0, 0.0).astype(BF16)

    part = LEVELS
    lane = iota((part, LANE), 1)
    of_field = [jnp.where(lane // 16 == f, 1.0, 0.0).astype(BF16) for f in range(nfield)]

    sub = pl.program_id(0) % (GROUP // part)

    def levels():
        def cell(a, t):
            if STEPS <= t < rows + STEPS:
                return plane(fields_ref, coefs, a, pl.ds(t - STEPS, part, stride=rows))
            side, at = (0, t) if t < STEPS else (1, t - rows - STEPS)
            return rim_ref[side, at, a]

        def strip(kind, t):
            return strip_ref[pl.ds(t * GROUP + sub * part, part), kind * LANE : (kind + 1) * LANE]

        for t in range(1, total - 1):
            at = slice(t * part, (t + 1) * part)
            for c, value in enumerate(weights_of(cell(nfield, t), cell(nfield + 1, t), cell(nfield + 2, t))):
                coef_ref[0, c, at] = value
            for c, value in enumerate(weights_of(strip(1, t), strip(2, t), strip(3, t))):
                coef_ref[1, c, at] = value
        for f in range(nfield):
            for t in range(total):
                state_ref[0, f, t * part : (t + 1) * part] = cell(f, t)

        state = {t: strip(0, t) for t in range(total)}
        for step in range(STEPS):
            inner = range(step + 1, total - 1 - step)
            for t in inner:
                narrow = state[t].astype(BF16)
                for f in range(nfield):
                    join_ref[step, f, t * part : (t + 1) * part] = narrow * of_field[f]
            if step < STEPS - 1:
                state = {
                    t: stepped(
                        [coef_ref[1, c, t * part : (t + 1) * part] for c in range(5)],
                        state[t],
                        pltpu.roll(state[t], LANE - 1, 1),
                        pltpu.roll(state[t], 1, 1),
                        state[t + 1],
                        state[t - 1],
                    )
                    for t in inner
                }

        def rows_of(step, by=0):
            return slice((step + 1 + by) * part, (total - 1 - step + by) * part)

        def neighbours(step, pair):
            at = rows_of(step)
            cells = [
                jnp.concatenate([state_ref[step % 2, f, at].astype(BF16), join_ref[step, f, at]], axis=1) for f in pair
            ]
            return mul(jnp.concatenate(cells, axis=0), shift_ref[...])

        turns = [(step, pair) for step in range(STEPS) for pair in ((0, 1), (2, 3))]
        ready = neighbours(*turns[0])
        for turn, (step, pair) in enumerate(turns):
            sides = ready
            if turn + 1 < len(turns):
                ready = neighbours(*turns[turn + 1])
            size = (total - 2 - 2 * step) * part
            cur = step % 2
            for u in range(step + 1, total - 1 - step):
                at, side = slice(u * part, (u + 1) * part), (u - step - 1) * part
                coef = [coef_ref[0, c, at] for c in range(5)]
                for n, f in enumerate(pair):
                    value = stepped(
                        coef,
                        state_ref[cur, f, at],
                        sides[n * size + side : n * size + side + part, :LANE],
                        sides[n * size + side : n * size + side + part, LANE:],
                        state_ref[cur, f, (u + 1) * part : (u + 2) * part],
                        state_ref[cur, f, (u - 1) * part : u * part],
                    )
                    if step < STEPS - 1:
                        state_ref[1 - cur, f, at] = value
                    else:
                        out_ref[f, pl.ds(u - STEPS, part, stride=rows), :] = value

    levels()


class Dynamics:
    def __init__(self, fields, coefs, rows, levels):
        self.args = (fields, *coefs)
        self.rows, self.levels = rows, levels
        nfield = fields.shape[0]
        planes = nfield + len(coefs)
        groups = pl.cdiv(levels, GROUP)
        self.grid = (groups,)
        self.planes = planes
        self.strip_rows = (rows + 2 * STEPS) * GROUP
        self.fields_spec = pl.BlockSpec((nfield, GROUP * rows, LANE), lambda i: (0, i, 0))
        self.arg_specs = [self.fields_spec] + [pl.BlockSpec((GROUP * rows, LANE), lambda i: (i, 0))] * 3
        self.rim_spec = pl.BlockSpec((STEPS, planes, GROUP, LANE), lambda i: (0, 0, i, 0))
        self.rim_shape = jax.ShapeDtypeStruct((STEPS, planes, groups * GROUP, LANE), BF16)
        self.strip_spec = pl.BlockSpec((self.strip_rows, LANE), lambda i: (0, 0))
        self.strip_shape = jax.ShapeDtypeStruct((self.strip_rows, LANE), BF16)

    def rims(self, start):
        def kernel(*refs):
            rim_kernel(*refs, rows=self.rows, levels=self.levels)

        return pl.pallas_call(
            kernel,
            grid=self.grid,
            in_specs=self.arg_specs,
            out_specs=[self.rim_spec, self.rim_spec],
            out_shape=[self.rim_shape, self.rim_shape],
            name="rims",
        )(self.args[0], *after(self.args[1:], start))

    def send_rims(self, low, high):
        size = lax.axis_size("lat")
        up = [(i, i + 1) for i in range(size - 1)]
        south = lax.ppermute(high, "lat", up)
        north = lax.ppermute(low, "lat", [(j, i) for i, j in up])
        return south, north

    def strips(self, south, north, start):
        def kernel(*refs):
            strip_kernel(*refs, rows=self.rows, levels=self.levels)

        south, north = after((south, north), start)
        return pl.pallas_call(
            kernel,
            grid=self.grid,
            in_specs=self.arg_specs + [self.rim_spec, self.rim_spec],
            out_specs=[self.strip_spec, self.strip_spec],
            out_shape=[self.strip_shape, self.strip_shape],
            scratch_shapes=[
                pltpu.VMEM((self.strip_rows, self.planes * LANE), BF16),
                pltpu.VMEM((self.strip_rows, 2 * LANE), F32),
            ],
            name="strips",
        )(*self.args, south, north)

    def send_strips(self, own_w, own_e):
        size = lax.axis_size("lon")
        around = [(i, (i + 1) % size) for i in range(size)]
        from_w = lax.ppermute(own_e, "lon", around)
        from_e = lax.ppermute(own_w, "lon", [(j, i) for i, j in around])
        return from_w, from_e

    def steps(self, first, count, rims, strips, start, state=None):
        def kernel(*refs):
            inputs = refs[:10]
            dynamics_kernel(*inputs, *refs[10 + (state is not None) :], rows=self.rows, first=first)

        fields = self.args[0]
        nfield = fields.shape[0]
        chunk = LEVELS * self.rows
        skip = first * (GROUP // LEVELS)
        fields_spec = pl.BlockSpec((nfield, chunk, LANE), lambda i: (0, i + skip, 0))
        coef_spec = pl.BlockSpec((chunk, LANE), lambda i: (i + skip, 0))
        rim_spec = pl.BlockSpec((STEPS, self.planes, LEVELS, LANE), lambda i: (0, 0, i + skip, 0))
        specs = [fields_spec] + [coef_spec] * 3 + [rim_spec] * 2 + [self.strip_spec] * 4
        operands = self.args + rims + after(strips, start)
        aliases = {}
        if state is not None:
            specs.append(pl.BlockSpec(memory_space=pl.ANY))
            aliases = {len(operands): 0}
            operands += (state,)
        cells = (self.rows + 2 * STEPS) * LEVELS
        return pl.pallas_call(
            kernel,
            grid=(count * (GROUP // LEVELS),),
            in_specs=specs,
            out_specs=fields_spec,
            out_shape=jax.ShapeDtypeStruct(fields.shape, F32),
            input_output_aliases=aliases,
            scratch_shapes=[
                pltpu.VMEM((2, STEPS, self.planes, LEVELS, LANE), F32),
                pltpu.VMEM((self.strip_rows, 4 * LANE), F32),
                pltpu.VMEM((2, 5, cells, LANE), F32),
                pltpu.VMEM((STEPS, nfield, cells, LANE), BF16),
                pltpu.VMEM((2, nfield, cells, LANE), F32),
                pltpu.VMEM((2 * LANE, 2 * LANE), BF16),
            ],
            cost_estimate=pl.CostEstimate(
                flops=fields.size * 60 * count // self.grid[0],
                transcendentals=0,
                bytes_accessed=fields.size * 11 * count // self.grid[0],
            ),
            name="dynamics",
        )(*operands)


def after(values, start):
    return lax.optimization_barrier((values, start))[0]


def exchange(array, axis):
    return lax.all_to_all(array, axis, split_axis=0, concat_axis=0, tiled=True)


def spread(piece):
    size = lax.axis_size("lat")
    other = lax.ppermute(piece, "lat", [(i, i ^ 1) for i in range(size)])
    both = jnp.concatenate([piece, other], axis=0)
    pieces = [both]
    for shift in range(1, size // 2):
        pieces.append(lax.ppermute(both, "lat", [(i, (i + 2 * shift) % size) for i in range(size)]))
    return pieces


def scattered(parts, start):
    size = parts.shape[0]
    core = lax.axis_index("lat") % 2
    pairs = parts.reshape((size // 2, 2) + parts.shape[1:])
    mine = lax.dynamic_index_in_dim(pairs, core, 1, keepdims=False)
    other = lax.dynamic_index_in_dim(pairs, 1 - core, 1, keepdims=False)
    other = lax.ppermute(other, "lat", [(i, i ^ 1) for i in range(size)])
    both = mine.astype(F32) + other.astype(F32)
    chips = size // 2
    chip = lax.axis_index("lat") // 2
    total = lax.dynamic_index_in_dim(both, chip, 0, keepdims=False)
    both = after(both.astype(BF16), start)
    for shift in range(1, chips):
        part = lax.dynamic_index_in_dim(both, (chip + shift) % chips, 0, keepdims=False)
        to = [(i, (i + 2 * shift) % size) for i in range(size)]
        total = total + lax.ppermute(part, "lat", to).astype(F32)
    return total


def shards(
    fields,
    courant_lon,
    courant_lat,
    diffusion,
    tend_cot,
    col_list,
    block_count,
    block_dest,
    w_in,
    w_mid,
    w_out,
):
    nfield, levels, rows, columns = fields.shape
    feat = nfield * levels
    hid_mid, hid_own = w_mid.shape[1:]
    nlat = lax.axis_size("lat")
    pad = -feat % LANE
    cuts = (
        (0, feat),
        (feat + pad, feat + pad + hid_mid),
        (feat + pad + hid_mid, 2 * feat + pad + hid_mid),
    )
    span = cuts[2][1] + pad

    coefs = [c.reshape(levels * rows, columns) for c in (courant_lon, courant_lat, diffusion)]
    window = Dynamics(fields.reshape(nfield, levels * rows, columns), coefs, rows, levels)

    nblock = block_dest.shape[-1]
    cols = col_list.reshape(nblock, 1, LANE)
    send_x, table = gather_first(block_dest, block_count, cols, fields.reshape(feat * rows, columns), feat, rows)
    recv_x = exchange(send_x, "lon")
    rest = jnp.zeros((pad, hid_own), BF16)
    own = jnp.concatenate([w_in[0], rest, w_mid[0], w_out[0], rest], axis=0).T
    pieces = spread(after(own, send_x))
    lat = lax.axis_index("lat")
    at = jnp.stack([lat // 2, lat % 2]).astype(jnp.int32)
    low, high = window.rims(send_x)
    south, north = window.send_rims(low, high)
    send_g = gather_columns(after(table, low), tend_cot.reshape(feat * rows, columns), feat, rows)
    recv_g = exchange(send_g, "lon")
    own_w, own_e = window.strips(south, north, send_g)
    from_w, from_e = window.send_strips(own_w, own_e)
    tend, a_one, a_two = physics_forward(at, after(recv_x, own_w), pieces, cuts)
    back_tend = exchange(tend, "lon")
    adj, grads = physics_backward(at, recv_x, recv_g, a_one, a_two, pieces, cuts)
    rims, strips = (south, north), (own_w, own_e, from_e, from_w)
    last = window.grid[0] - 1
    state = window.steps(last, 1, rims, strips, adj)
    back_adj = exchange(after(adj, back_tend), "lon")
    state = window.steps(0, last, rims, strips, back_tend, state)
    summed = scattered(grads.reshape(nlat, hid_own, span), back_tend).T
    grad_in, grad_mid, grad_out = (summed[a:b][None] for a, b in cuts)

    new_fields = scatter_columns(table, back_tend, rows, state.reshape(feat * rows, columns))
    adjoint = scatter_columns(table, back_adj, rows)
    return (new_fields.reshape(fields.shape), adjoint.reshape(fields.shape), grad_in, grad_mid, grad_out)


def solution(mesh):
    return jax.shard_map(
        shards,
        mesh=mesh,
        in_specs=(
            P(None, None, "lat", "lon"),
            P(None, "lat", "lon"),
            P(None, "lat", "lon"),
            P(None, "lat", "lon"),
            P(None, None, "lat", "lon"),
            P("lat", "lon", None),
            P("lat", "lon", None),
            P("lat", "lon", None),
            P("lon", None, "lat"),
            P("lon", None, "lat"),
            P("lon", None, "lat"),
        ),
        out_specs=(
            P(None, None, "lat", "lon"),
            P(None, None, "lat", "lon"),
            P("lon", None, "lat"),
            P("lon", None, "lat"),
            P("lon", None, "lat"),
        ),
        check_vma=False,
    )
```
